128 devices in a mesh: section: 8 (over y, z_lo), dp: 16 (over z_hi, x, core).
Axes of the slice: x: 4, y: 4, z: 4 (z_hi: 2, z_lo: 2; z = z_hi * 2 + z_lo), core: 2. Of those that a mesh axis runs over, the one named last changes fastest.
Arguments:
- images: bfloat16 [32, 16, 16, 768], P('dp'), may hold values from -6 to 6
- roster: int32 [16, 2], P('dp'), may hold values from 0 to 1, each once within a row
- cotangent: bfloat16 [32, 16, 16, 768], P('dp'), may hold values from -6 to 6
- depth_kernel: bfloat16 [8, 7, 7, 768], P('section'), may hold values from -0.875 to 0.875
- up_weight: bfloat16 [8, 768, 3072], P('section'), may hold values from -0.21875 to 0.21875
- down_weight: bfloat16 [8, 3072, 768], P('section'), may hold values from -0.109375 to 0.109375
- layer_scale: float32 [8, 768], P('section'), may hold values from 0.3 to 1
- master: float32 [8, 55744, 128], P('section', 'dp'), may hold values from -0.75 to 0.75
- first_moment: float32 [8, 55744, 128], P('section', 'dp'), may hold values from -6 to 6
- second_moment: float32 [8, 55744, 128], P('section', 'dp'), may hold values from 0.05 to 5
- bucket_bounds: int32 [8, 49], P('section'), may hold values from 0 to 37168, as said below
- bucket_owner: int32 [8, 48], P('section'), may hold values from 0 to 15, as said below
Outputs:
- section_outputs: bfloat16 [8, 32, 16, 16, 768], P('section', 'dp')
- new_master: float32 [8, 55744, 128], P('section', 'dp')
- new_first_moment: float32 [8, 55744, 128], P('section', 'dp')
- new_second_moment: float32 [8, 55744, 128], P('section', 'dp')
The draws below stay inside these ranges and needn't reach their ends.
Inputs may be any that keep to these rules, and one draw needn't show every extreme that they name: `roster`: each row names every slot once. `bucket_bounds`: in each block's row the bounds never fall, the first is 0 and the last is 37168. `bucket_owner`: in each block every owner is named by 3 buckets; the buckets of one owner hold at most 3484 rows together, and some owner holds exactly 3484.
All inputs are finite; a program needn't handle non-finite values.
Results may differ from the reference program's by a relative error of at most 0.028.
Values may be sent and summed in bfloat16 or wider, within the bound.
No kernel may reach another device: no remote copies, remote signals or barrier semaphores. Data moves between devices by JAX's collectives and lax.ppermute only.
A program may use at most 128 MiB of HBM per device.

```python
import math
import jax
import jax.numpy as jnp
from jax import lax

C = 768
HID = 3072
KS = 7
H = 16
W = 16
MICRO = 2
GRAN = 128
BPO = 3
SECTIONS = 8
REPLICAS = 16
IMAGES = 32
NROWS = 37164
AVG = 2323
UNITS = 37168
SPREAD = 1161
CAPR = 3484
NB = 48


def bucket_plan(key):

    def one_section(section_key):
        subkeys = jax.random.split(section_key, 6)
        pair_count = REPLICAS // 2
        extra_rows = jax.random.randint(subkeys[0], (pair_count,), 0, SPREAD + 1)
        forced = jax.random.randint(subkeys[1], (), 0, pair_count)
        extra_rows = jnp.where(jnp.arange(pair_count) == forced, SPREAD, extra_rows)
        flip_sign = 1 - 2 * jax.random.randint(subkeys[2], (pair_count,), 0, 2)
        owner_loads = jnp.stack([AVG + flip_sign * extra_rows, AVG - flip_sign * extra_rows], axis=1).reshape(-1)
        owner_loads = owner_loads[jax.random.permutation(subkeys[3], REPLICAS)]
        weights = jax.random.randint(subkeys[4], (REPLICAS, BPO), 1, 5)
        running = jnp.cumsum(weights, axis=1)
        cut_points = owner_loads[:, None] * running // running[:, -1:]
        bucket_sizes = cut_points - jnp.concatenate([jnp.zeros((REPLICAS, 1), cut_points.dtype), cut_points[:, :-1]], axis=1)
        bucket_order = jax.random.permutation(subkeys[5], NB)
        flat_sizes = bucket_sizes.reshape(-1)[bucket_order]
        owners = (jnp.arange(NB) // BPO)[bucket_order]
        bounds = jnp.concatenate([jnp.zeros((1,), flat_sizes.dtype), jnp.cumsum(flat_sizes)])
        return (bounds.astype(jnp.int32), owners.astype(jnp.int32))
    return jax.vmap(one_section)(jax.random.split(jax.random.fold_in(key, 7), SECTIONS))


def draw_bucket_bounds(key, part):
    return bucket_plan(key)[0]


def draw_bucket_owner(key, part):
    return bucket_plan(key)[1]


def block_scale(rng, extent, cuts, low, top_value):
    def one(position, parts):
        draws = jax.random.uniform(jax.random.fold_in(jax.random.fold_in(rng, 6), position), (parts,), jnp.float32, low / len(cuts), top_value / len(cuts))
        return jnp.repeat(jnp.exp(draws), extent[position] // parts).reshape((-1,) + (1,) * (len(extent) - position - 1))

    gain = one(*cuts[0])
    for cut in cuts[1:]:
        gain = gain * one(*cut)
    return gain


def gaussian(stream_key, shape, deviation, bound, pieces=(), held_as=jnp.bfloat16):
    array = jax.random.normal(stream_key, shape, jnp.float32) * deviation
    if len(pieces) > 0:
        array = block_scale(stream_key, shape, pieces, -0.22, 0.18) * array
    return jnp.clip(array, min=-bound, max=bound).astype(held_as)


def setup_inputs(seed: int = 0) -> dict:
    splits = jax.random.split(jax.random.key(seed), 13)
    images = gaussian(splits[0], (IMAGES, H, W, C), 1.0, 6.0, ((0, 16),))
    roster = jax.vmap(lambda own: jax.random.permutation(own, MICRO))(jax.random.split(splits[1], REPLICAS)).reshape((REPLICAS, MICRO)).astype(jnp.int32)
    cotangent = gaussian(splits[2], (IMAGES, H, W, C), 1.0, 6.0, ((0, 16),))
    depth_kernel = gaussian(splits[3], (SECTIONS, KS, KS, C), (KS * KS) ** -0.5, 0.875, ((0, 8),))
    up_weight = gaussian(splits[4], (SECTIONS, C, HID), C ** -0.5, 0.21875, ((0, 8),))
    down_weight = gaussian(splits[5], (SECTIONS, HID, C), HID ** -0.5, 0.109375, ((0, 8),))
    layer_scale = jnp.clip(jnp.exp(math.log(1.0) - 1.2039728 * jax.random.uniform(splits[6], (SECTIONS, C), jnp.float32) ** block_scale(splits[6], (SECTIONS, C), ((0, 8),), -0.2, 0.2)), 0.3, 1.0)
    master = gaussian(splits[7], (SECTIONS, REPLICAS * CAPR, GRAN), 0.05, 0.75, ((0, 8), (1, 16)), jnp.float32)
    first_moment = gaussian(splits[8], (SECTIONS, REPLICAS * CAPR, GRAN), 0.5, 6.0, ((0, 8), (1, 16)), jnp.float32)
    second_moment = jnp.clip(jnp.exp(math.log(5.0) - 4.6051702 * jax.random.uniform(splits[9], (SECTIONS, REPLICAS * CAPR, GRAN), jnp.float32) ** block_scale(splits[9], (SECTIONS, REPLICAS * CAPR, GRAN), ((0, 8), (1, 16)), -0.2, 0.2)), 0.05, 5.0)
    bucket_bounds = draw_bucket_bounds(jax.random.fold_in(splits[12], 71), 0)
    bucket_owner = draw_bucket_owner(jax.random.fold_in(splits[12], 71), 0)
    return dict(images=images, roster=roster, cotangent=cotangent, depth_kernel=depth_kernel, up_weight=up_weight, down_weight=down_weight, layer_scale=layer_scale, master=master, first_moment=first_moment, second_moment=second_moment, bucket_bounds=bucket_bounds, bucket_owner=bucket_owner)


beta_one = 0.9
beta_two = 0.95
learn_rate = 0.01
decay_rate = 0.1
adam_eps = 1e-08
norm_eps = 1e-06
first_fix = 1.0 - 0.9 ** 10
second_fix = 1.0 - 0.95 ** 10

def depthwise(inputs, kernel):
    reach = (kernel.shape[0] - 1) // 2
    return lax.conv_general_dilated(inputs, kernel[:, :, None, :], (1, 1), ((reach, reach), (reach, reach)), dimension_numbers=('NHWC', 'HWIO', 'NHWC'), feature_group_count=inputs.shape[-1], preferred_element_type=jnp.float32)

def gelu_slope(values):
    cumulative = 0.5 * (1.0 + lax.erf(values * 0.7071067811865476))
    return cumulative + values * jnp.exp(-0.5 * values * values) * 0.3989422804014327

def normalize(conv_rows):
    centred = conv_rows - lax.optimization_barrier(jnp.mean(conv_rows, axis=-1, keepdims=True))
    inv_std = lax.rsqrt(lax.optimization_barrier(jnp.mean(centred * centred, axis=-1, keepdims=True)) + norm_eps)
    return (centred * inv_std, inv_std)

def block_forward(block_in, kernel, up_matrix, down_matrix, scale_row):
    channels = block_in.shape[-1]
    conv_rows = depthwise(block_in, kernel).reshape(-1, channels)
    normed_f, inv_std = normalize(conv_rows)
    normed = normed_f.astype(jnp.bfloat16)
    hidden_pre = jnp.dot(normed, up_matrix, preferred_element_type=jnp.float32)
    hidden = jax.nn.gelu(hidden_pre, approximate=False).astype(jnp.bfloat16)
    branch = jnp.dot(hidden, down_matrix, preferred_element_type=jnp.float32)
    block_out = block_in.reshape(-1, channels).astype(jnp.float32) + scale_row * branch
    return (block_out.astype(jnp.bfloat16).reshape(block_in.shape), conv_rows, hidden_pre, branch)

def block_backward(grad_out, block_in, conv_rows, hidden_pre, branch, kernel, up_matrix, down_matrix, scale_row):
    channels = block_in.shape[-1]
    out_rows = grad_out.reshape(-1, channels).astype(jnp.float32)
    scaled = (out_rows * scale_row).astype(jnp.bfloat16)
    scale_terms = out_rows * branch
    hidden = jax.nn.gelu(hidden_pre, approximate=False).astype(jnp.bfloat16)
    grad_hidden = lax.dot_general(scaled, down_matrix, (((1,), (1,)), ((), ())), preferred_element_type=jnp.float32)
    grad_pre = (grad_hidden * gelu_slope(hidden_pre)).astype(jnp.bfloat16)
    normed_f, inv_std = normalize(conv_rows)
    normed = normed_f.astype(jnp.bfloat16)
    grad_normed = lax.dot_general(grad_pre, up_matrix, (((1,), (1,)), ((), ())), preferred_element_type=jnp.float32)
    grad_conv = inv_std * (grad_normed - lax.optimization_barrier(jnp.mean(grad_normed, axis=-1, keepdims=True)) - normed_f * lax.optimization_barrier(jnp.mean(grad_normed * normed_f, axis=-1, keepdims=True)))
    grad_conv = grad_conv.astype(jnp.bfloat16).reshape(block_in.shape)
    back_conv = depthwise(grad_conv, kernel[::-1, ::-1])
    grad_in = (out_rows + back_conv.reshape(-1, channels)).astype(jnp.bfloat16).reshape(block_in.shape)
    return (grad_in, scaled, hidden, grad_pre, normed, grad_conv, scale_terms)

def owner_slots(bounds, owners, owner_id, slot_count, empty_row):
    lengths = bounds[1:] - bounds[:-1]
    mine = (owners == owner_id).astype(jnp.int32)
    taken = lengths * mine
    offsets = jnp.cumsum(taken) - taken
    slot_ids = jnp.arange(slot_count, dtype=jnp.int32)[:, None]
    hits = (mine[None, :] > 0) & (slot_ids >= offsets[None, :]) & (slot_ids < (offsets + lengths)[None, :])
    found = lax.optimization_barrier(jnp.sum(jnp.where(hits, bounds[:-1][None, :] + slot_ids - offsets[None, :], 0), axis=1))
    return jnp.where(jnp.any(hits, axis=1), found, empty_row).astype(jnp.int32)

def kernel_grads(block_in, grad_conv, kernel, replica_count):
    reach = (kernel.shape[0] - 1) // 2
    height, breadth, channels = (block_in.shape[1], block_in.shape[2], block_in.shape[3])
    padded = jnp.pad(block_in.astype(jnp.float32), ((0, 0), (reach, reach), (reach, reach), (0, 0)))
    grad_values = grad_conv.astype(jnp.float32)
    columns = []
    for row_shift in range(2 * reach + 1):
        for col_shift in range(2 * reach + 1):
            window = padded[:, row_shift:row_shift + height, col_shift:col_shift + breadth, :]
            product = (window * grad_values).reshape(replica_count, -1, channels)
            columns.append(lax.optimization_barrier(jnp.sum(product, axis=1)))
    return jnp.stack(columns, axis=1)

def reference(images, roster, cotangent, depth_kernel, up_weight, down_weight, layer_scale, master, first_moment, second_moment, bucket_bounds, bucket_owner):
    picks = (jnp.arange(REPLICAS, dtype=jnp.int32)[:, None] * MICRO + roster).reshape(-1)
    block_in = images[picks]
    inputs = []
    outputs = []
    for section_id in range(SECTIONS):
        inputs.append(block_in)
        block_in = block_forward(block_in, depth_kernel[section_id], up_weight[section_id], down_weight[section_id], layer_scale[section_id])[0]
        outputs.append(block_in)
    section_outputs = jnp.stack(outputs)
    grad_out = cotangent
    per_rows = MICRO * H * W
    masters = []
    firsts = []
    seconds = []
    for section_id in reversed(range(SECTIONS)):
        kernel = depth_kernel[section_id]
        section_in = inputs[section_id]
        forward_parts = block_forward(section_in, kernel, up_weight[section_id], down_weight[section_id], layer_scale[section_id])
        grad_in, scaled, hidden, grad_pre, normed, grad_conv, scale_terms = block_backward(grad_out, section_in, forward_parts[1], forward_parts[2], forward_parts[3], kernel, up_weight[section_id], down_weight[section_id], layer_scale[section_id])
        grad_out = grad_in
        scale_grad = lax.optimization_barrier(jnp.sum(scale_terms.reshape(REPLICAS, per_rows, C), axis=1))
        down_grad = jnp.einsum('rph,rpc->rhc', hidden.astype(jnp.float32).reshape(REPLICAS, per_rows, HID), scaled.astype(jnp.float32).reshape(REPLICAS, per_rows, C))
        up_grad = jnp.einsum('rpc,rph->rch', normed.astype(jnp.float32).reshape(REPLICAS, per_rows, C), grad_pre.astype(jnp.float32).reshape(REPLICAS, per_rows, HID))
        kernel_grad = kernel_grads(section_in, grad_conv, kernel, REPLICAS)
        flat_grad = jnp.concatenate([kernel_grad.reshape(REPLICAS, -1), up_grad.reshape(REPLICAS, -1), down_grad.reshape(REPLICAS, -1), scale_grad], axis=1).astype(jnp.bfloat16)
        flat_grad = lax.optimization_barrier(flat_grad).astype(jnp.float32)
        summed = lax.optimization_barrier(jnp.sum(flat_grad, axis=0)) / REPLICAS
        grad_rows = jnp.concatenate([summed.reshape(NROWS, GRAN), jnp.zeros((UNITS - NROWS + 1, GRAN), summed.dtype)], axis=0)
        slot_rows = jax.vmap(lambda owner_id: owner_slots(bucket_bounds[section_id], bucket_owner[section_id], owner_id, CAPR, UNITS))(jnp.arange(REPLICAS, dtype=jnp.int32)).reshape(-1)
        grad = grad_rows[slot_rows]
        new_first = beta_one * first_moment[section_id] + (1.0 - beta_one) * grad
        new_second = beta_two * second_moment[section_id] + (1.0 - beta_two) * grad * grad
        update = new_first / first_fix / (jnp.sqrt(new_second / second_fix) + adam_eps) + decay_rate * master[section_id]
        masters.append(master[section_id] - learn_rate * update)
        firsts.append(new_first)
        seconds.append(new_second)
    new_master = jnp.stack(masters[::-1])
    new_first_moment = jnp.stack(firsts[::-1])
    new_second_moment = jnp.stack(seconds[::-1])
    return (section_outputs, new_master, new_first_moment, new_second_moment)
```

```python
import functools

import jax
import jax.numpy as jnp
from jax import lax
from jax.experimental import pallas as pl
from jax.experimental.pallas import tpu as pltpu
from jax.sharding import PartitionSpec as P

beta_one = 0.9
beta_two = 0.95
learn_rate = 0.01
decay_rate = 0.1
adam_eps = 1e-08
norm_eps = 1e-06
first_fix = 1.0 - 0.9**10
second_fix = 1.0 - 0.95**10

LANES = 128
MARGIN = 8
STEP = 64
F32 = jnp.float32
BF16 = jnp.bfloat16
ANY = pl.BlockSpec(memory_space=pl.ANY)
SMEM = pl.BlockSpec(memory_space=pltpu.SMEM)
VMEM = pl.BlockSpec(memory_space=pltpu.VMEM)
PARAMS = pltpu.CompilerParams(vmem_limit_bytes=56 * 1024 * 1024)


def rolled(count):
    def wrap(fn):
        lax.fori_loop(0, count, lambda i, c: (fn(i), c)[1], 0)

    return wrap


def pad_map(pad, image, reach, height, breadth):
    chunks = pad.shape[0]
    for c in range(chunks):
        for r in range(pad.shape[1]):
            if r < reach or r >= reach + height:
                pad[c, r] = jnp.zeros(pad.shape[2:], F32)
            else:
                pad[c, r, :MARGIN] = jnp.zeros((MARGIN, LANES), F32)
                pad[c, r, MARGIN + breadth :] = jnp.zeros((MARGIN, LANES), F32)
                pad[c, r, MARGIN : MARGIN + breadth] = image[
                    (r - reach) * breadth : (r - reach + 1) * breadth,
                    c * LANES : (c + 1) * LANES,
                ].astype(F32)


def depthwise(pad, taps, result, side, height, breadth, flip):
    reach = (side - 1) // 2
    halves = breadth // 8

    @rolled(pad.shape[0])
    def _(c):
        sums = [[None] * halves for _ in range(height)]
        for b in range(side):
            weights = []
            for a in range(side):
                t = a * side + b
                t = side * side - 1 - t if flip else t
                weights.append(jnp.broadcast_to(taps[c, pl.ds(t, 1), :], (8, LANES)))
            for r in range(height + 2 * reach):
                for w in range(halves):
                    value = pad[c, r, pl.ds(MARGIN - reach + b + 8 * w, 8), :]
                    for a in range(side):
                        i = r - a
                        if 0 <= i < height:
                            term = value * weights[a]
                            sums[i][w] = term if sums[i][w] is None else sums[i][w] + term
        columns = pl.ds(pl.multiple_of(c * LANES, LANES), LANES)
        for i in range(height):
            for w in range(halves):
                result[pl.ds(i * breadth + 8 * w, 8), columns] = sums[i][w]


def forward_kernel(
    dims, sc, xr, images, taps, scale, up, down, *refs
):
    side, height, breadth, width = dims
    out_o, x_o, n_o, istd_o, hid_o, slope_o, branch_o, y = refs[7:15]
    xv, pad, conv, nv, iv, upv, downv, hv, sv, acc, yv, sems = refs[15:]
    positions, channels = xv.shape
    reach = (side - 1) // 2

    @pl.when(sc[0] > 0)
    def _():
        slot = sc[2]
        up_in = pltpu.make_async_copy(up, upv, sems.at[0])
        down_in = pltpu.make_async_copy(down, downv, sems.at[1])

        @pl.when(sc[1] > 0)
        def _():
            cp = pltpu.make_async_copy(images.at[sc[3]], xv, sems.at[2])
            cp.start()
            up_in.start()
            down_in.start()
            cp.wait()

        @pl.when(sc[1] == 0)
        def _():
            cp = pltpu.make_async_copy(xr, xv, sems.at[2])
            cp.start()
            up_in.start()
            down_in.start()
            cp.wait()

        x_out = pltpu.make_async_copy(xv, x_o.at[slot], sems.at[3])
        x_out.start()
        pad_map(pad, xv, reach, height, breadth)
        depthwise(pad, taps, conv, side, height, breadth, False)
        block = 64
        for p in range(0, positions, block):
            rows = conv[p : p + block, :]
            centred = rows - jnp.mean(rows, axis=-1, keepdims=True)
            inv_std = lax.rsqrt(jnp.mean(centred * centred, axis=-1, keepdims=True) + norm_eps)
            nv[p : p + block, :] = (centred * inv_std).astype(BF16)
            iv[p : p + block, :] = jnp.broadcast_to(inv_std, (block, LANES))
        n_out = pltpu.make_async_copy(nv, n_o.at[slot], sems.at[4])
        n_out.start()
        i_out = pltpu.make_async_copy(iv, istd_o.at[slot], sems.at[5])
        i_out.start()
        up_in.wait()
        down_in.wait()
        step = 512
        for k in range(0, width, step):
            pre = jnp.dot(nv[...], upv[:, k : k + step], preferred_element_type=F32)
            cdf = 0.5 * (1.0 + lax.erf(pre * 0.7071067811865476))
            hidden = (pre * cdf).astype(BF16)
            hv[:, k : k + step] = hidden
            bell = jnp.exp(-0.5 * pre * pre) * 0.3989422804014327
            sv[:, k : k + step] = (cdf + pre * bell).astype(BF16)
            part = jnp.dot(hidden, downv[k : k + step, :], preferred_element_type=F32)
            if k == 0:
                acc[...] = part
            else:
                acc[...] += part
        yv[...] = (xv[...].astype(F32) + scale[...] * acc[...]).astype(BF16)
        y_out = pltpu.make_async_copy(yv, y, sems.at[6])
        y_out.start()
        o_out = pltpu.make_async_copy(yv, out_o.at[slot], sems.at[7])
        o_out.start()
        h_out = pltpu.make_async_copy(hv, hid_o.at[slot], sems.at[8])
        h_out.start()
        s_out = pltpu.make_async_copy(sv, slope_o.at[slot], sems.at[9])
        s_out.start()
        b_out = pltpu.make_async_copy(acc, branch_o.at[slot], sems.at[10])
        b_out.start()
        for cp in (x_out, n_out, i_out, y_out, o_out, h_out, s_out, b_out):
            cp.wait()


def backward_kernel(
    dims, sc, gr, cotangent, taps, scale, up, down, n_i, istd_i, slope_i, *refs
):
    side, height, breadth, width = dims
    go_o, gp_o, gc_o, g_in = refs[3:7]
    gv, pad, conv, nv, iv, upv, downv, sv, gpv, acc, scaled, gcv, yv, sems = refs[7:]
    positions, channels = gv.shape
    reach = (side - 1) // 2

    @pl.when(sc[0] > 0)
    def _():
        slot = sc[2]
        down_in = pltpu.make_async_copy(down, downv, sems.at[0])
        up_in = pltpu.make_async_copy(up, upv, sems.at[1])
        s_in = pltpu.make_async_copy(slope_i.at[slot], sv, sems.at[3])
        n_in = pltpu.make_async_copy(n_i.at[slot], nv, sems.at[4])
        i_in = pltpu.make_async_copy(istd_i.at[slot], iv, sems.at[5])

        def begin(source):
            cp = pltpu.make_async_copy(source, gv, sems.at[2])
            cp.start()
            down_in.start()
            s_in.start()
            up_in.start()
            n_in.start()
            i_in.start()
            cp.wait()

        @pl.when(sc[1] > 0)
        def _():
            begin(cotangent.at[slot])

        @pl.when(sc[1] == 0)
        def _():
            begin(gr)

        go_out = pltpu.make_async_copy(gv, go_o.at[slot], sems.at[6])
        go_out.start()
        scaled[...] = (gv[...].astype(F32) * scale[...]).astype(BF16)
        down_in.wait()
        s_in.wait()
        up_in.wait()
        step = 512
        across = (((1,), (1,)), ((), ()))
        for k in range(0, width, step):
            grad_hidden = lax.dot_general(
                scaled[...], downv[k : k + step, :], across, preferred_element_type=F32
            )
            grad_pre = (grad_hidden * sv[:, k : k + step].astype(F32)).astype(BF16)
            gpv[:, k : k + step] = grad_pre
            part = lax.dot_general(
                grad_pre, upv[:, k : k + step], across, preferred_element_type=F32
            )
            if k == 0:
                acc[...] = part
            else:
                acc[...] += part
        gp_out = pltpu.make_async_copy(gpv, gp_o.at[slot], sems.at[7])
        gp_out.start()
        n_in.wait()
        i_in.wait()
        block = 64
        for p in range(0, positions, block):
            rows = acc[p : p + block, :]
            normed = nv[p : p + block, :].astype(F32)
            mean = jnp.mean(rows, axis=-1, keepdims=True)
            slant = jnp.mean(rows * normed, axis=-1, keepdims=True)
            gcv[p : p + block, :] = (
                iv[p : p + block, :1] * (rows - mean - normed * slant)
            ).astype(BF16)
        gc_out = pltpu.make_async_copy(gcv, gc_o.at[slot], sems.at[8])
        gc_out.start()

        @pl.when(sc[3] > 0)
        def _():
            pad_map(pad, gcv, reach, height, breadth)
            depthwise(pad, taps, conv, side, height, breadth, True)
            yv[...] = (gv[...].astype(F32) + conv[...]).astype(BF16)
            cp = pltpu.make_async_copy(yv, g_in, sems.at[9])
            cp.start()
            cp.wait()

        for cp in (go_out, gp_out, gc_out):
            cp.wait()


def weight_kernel(
    dims, bounds, owners, scale, x_i, n_i, hid_i, branch_i, go_i, gp_i, gc_i, slots_o, *refs
):
    side, height, breadth, width, real_rows, owner_count, buckets = dims
    (xv, nv, hv, bv, gv, gpv, gcv, scaled, pad, flat, stage, ready, starts, lengths, counts, sems) = refs
    micro, positions, channels = x_i.shape
    reach = (side - 1) // 2
    chunks = channels // LANES
    rows = micro * positions
    tap_rows = side * side * chunks
    up_rows = channels * (width // LANES)
    down_base = tap_rows + up_rows
    scale_base = down_base + up_rows
    copies = []
    for q, (src, dst) in enumerate(
        ((n_i, nv), (gp_i, gpv), (go_i, gv), (hid_i, hv), (x_i, xv), (gc_i, gcv), (branch_i, bv))
    ):
        for m in range(micro):
            cp = pltpu.make_async_copy(
                src.at[m], dst.at[pl.ds(m * positions, positions)], sems.at[q * micro + m]
            )
            cp.start()
            copies.append(cp)
    for d in range(owner_count):
        counts[d] = 0

    @rolled(buckets)
    def _(b):
        d = owners[b]
        at = d * (buckets // owner_count) + counts[d]
        starts[at] = bounds[b]
        lengths[at] = bounds[b + 1] - bounds[b]
        counts[d] = counts[d] + 1

    for cp in copies:
        cp.wait()
    along = (((0,), (0,)), ((), ()))
    scaled[...] = (gv[...].astype(F32) * scale[...]).astype(BF16)
    for j in range(0, width // LANES, 2):
        part = lax.dot_general(
            nv[...], gpv[:, j * LANES : (j + 2) * LANES], along, preferred_element_type=F32
        )
        for q in range(2):
            flat[pl.ds(tap_rows + j + q, channels, stride=width // LANES), :] = part[
                :, q * LANES : (q + 1) * LANES
            ]
    for j in range(0, chunks, 2):
        part = lax.dot_general(
            hv[...], scaled[:, j * LANES : (j + 2) * LANES], along, preferred_element_type=F32
        )
        for q in range(2):
            flat[pl.ds(down_base + j + q, width, stride=chunks), :] = part[
                :, q * LANES : (q + 1) * LANES
            ]
    terms = jnp.sum(gv[...].astype(F32) * bv[...], axis=0, keepdims=True)
    for c in range(chunks):
        flat[pl.ds(scale_base + c, 1), :] = terms[:, c * LANES : (c + 1) * LANES]
    tail = flat.shape[0] - scale_base - chunks
    flat[pl.ds(scale_base + chunks, tail), :] = jnp.zeros((tail, LANES), F32)
    halves = breadth // 8
    for m in range(micro):
        pad_map(pad, xv.at[pl.ds(m * positions, positions)], reach, height, breadth)

        @rolled(chunks)
        def _(c):
            columns = pl.ds(pl.multiple_of(c * LANES, LANES), LANES)
            grads = [
                gcv[pl.ds(m * positions + 16 * i, 16), columns].astype(F32)
                for i in range(positions // 16)
            ]
            for b in range(side):
                sums = [None] * side
                for r in range(reach, height + reach):
                    for w in range(halves):
                        value = pad[c, r, pl.ds(MARGIN - reach + b + 8 * w, 8), :]
                        for a in range(side):
                            i = r - a
                            if 0 <= i < height:
                                p = i * breadth + 8 * w
                                term = value * grads[p // 16][p % 16 : p % 16 + 8]
                                sums[a] = term if sums[a] is None else sums[a] + term
                for a in range(side):
                    total = jnp.sum(sums[a], axis=0, keepdims=True)
                    at = pl.ds((a * side + b) * chunks + c, 1)
                    if m == 0:
                        flat[at, :] = total
                    else:
                        flat[at, :] += total

    share = ready.shape[1]

    def out_copy(d, q):
        return pltpu.make_async_copy(ready.at[q], slots_o.at[d], sems.at[7 * micro + q])

    @rolled(owner_count)
    def _(d):
        q = lax.rem(d, 2)
        offset = 0
        for k in range(buckets // owner_count):
            at = d * (buckets // owner_count) + k
            start, length = starts[at], lengths[at]
            here = offset

            def move(i, c, start=start, here=here):
                stage[pl.ds(here + STEP * i, STEP), :] = flat[pl.ds(start + STEP * i, STEP), :]
                return c

            lax.fori_loop(0, lax.div(length + STEP - 1, STEP), move, 0)
            offset = offset + length

        def clear(i, c):
            stage[pl.ds(offset + STEP * i, STEP), :] = jnp.zeros((STEP, LANES), F32)
            return c

        lax.fori_loop(0, lax.div(share - offset + STEP - 1, STEP), clear, 0)

        @pl.when(d >= 2)
        def _():
            out_copy(d - 2, q).wait()

        ready[q] = stage[:share, :].astype(BF16)
        out_copy(d, q).start()

    for d in range(owner_count - 2, owner_count):
        out_copy(d, d % 2).wait()


def adam_kernel(count, replicas, g_i, m_i, f_i, s_i, m_o, f_o, s_o, grads):
    @pl.when(pl.program_id(0) == 0)
    def _():
        grads[...] = g_i[...].astype(F32) * (1.0 / replicas)

    base = pl.program_id(0) * (4 * count)
    for k in range(count):
        grad = grads[pl.ds(base + 4 * k, 4), :]
        new_first = beta_one * f_i[k] + (1.0 - beta_one) * grad
        new_second = beta_two * s_i[k] + (1.0 - beta_two) * grad * grad
        update = (
            new_first / first_fix / (jnp.sqrt(new_second / second_fix) + adam_eps)
            + decay_rate * m_i[k]
        )
        m_o[k] = m_i[k] - learn_rate * update
        f_o[k] = new_first
        s_o[k] = new_second


def blank(shapes):
    def kernel(*refs):
        pass

    return pl.pallas_call(
        kernel, out_shape=shapes, out_specs=[ANY] * len(shapes), name="blank"
    )()


def body(
    images,
    roster,
    cotangent,
    depth_kernel,
    up_weight,
    down_weight,
    layer_scale,
    master,
    first_moment,
    second_moment,
    bucket_bounds,
    bucket_owner,
):
    sections = lax.axis_size("section")
    replicas = lax.axis_size("dp")
    section = lax.axis_index("section")
    micro, height, breadth, channels = images.shape
    side = depth_kernel.shape[1]
    width = up_weight.shape[2]
    positions = height * breadth
    chunks = channels // LANES
    up, down = up_weight[0], down_weight[0]
    taps = (
        depth_kernel[0].astype(F32).reshape(side * side, chunks, LANES).transpose(1, 0, 2)
    )
    images = images.reshape(micro, positions, channels)
    cotangent = cotangent.reshape(micro, positions, channels)
    sds = jax.ShapeDtypeStruct
    act = sds((micro, positions, channels), BF16)
    wide = sds((micro, positions, width), BF16)
    one = sds((positions, channels), BF16)
    spread = sds((micro, positions, LANES), F32)
    full = sds((micro, positions, channels), F32)
    pad_shape = (chunks, height + side - 1, breadth + 2 * MARGIN, LANES)
    dims = (side, height, breadth, width)

    kept = (act, act, act, spread, wide, wide, full)
    forward_call = pl.pallas_call(
        functools.partial(forward_kernel, dims),
        out_shape=(*kept, one),
        in_specs=[SMEM, ANY, ANY, VMEM, VMEM, ANY, ANY] + [ANY] * len(kept),
        out_specs=[ANY] * (len(kept) + 1),
        input_output_aliases={7 + q: q for q in range(len(kept))},
        scratch_shapes=[
            pltpu.VMEM((positions, channels), BF16),
            pltpu.VMEM(pad_shape, F32),
            pltpu.VMEM((positions, channels), F32),
            pltpu.VMEM((positions, channels), BF16),
            pltpu.VMEM((positions, LANES), F32),
            pltpu.VMEM((channels, width), BF16),
            pltpu.VMEM((width, channels), BF16),
            pltpu.VMEM((positions, width), BF16),
            pltpu.VMEM((positions, width), BF16),
            pltpu.VMEM((positions, channels), F32),
            pltpu.VMEM((positions, channels), BF16),
            pltpu.SemaphoreType.DMA((11,)),
        ],
        compiler_params=PARAMS,
        name="block_forward",
    )
    saved = (act, wide, act)
    backward_call = pl.pallas_call(
        functools.partial(backward_kernel, dims),
        out_shape=(*saved, one),
        in_specs=[SMEM, ANY, ANY, VMEM, VMEM, ANY, ANY, ANY, ANY, ANY] + [ANY] * len(saved),
        out_specs=[ANY] * (len(saved) + 1),
        input_output_aliases={10 + q: q for q in range(len(saved))},
        scratch_shapes=[
            pltpu.VMEM((positions, channels), BF16),
            pltpu.VMEM(pad_shape, F32),
            pltpu.VMEM((positions, channels), F32),
            pltpu.VMEM((positions, channels), BF16),
            pltpu.VMEM((positions, LANES), F32),
            pltpu.VMEM((channels, width), BF16),
            pltpu.VMEM((width, channels), BF16),
            pltpu.VMEM((positions, width), BF16),
            pltpu.VMEM((positions, width), BF16),
            pltpu.VMEM((positions, channels), F32),
            pltpu.VMEM((positions, channels), BF16),
            pltpu.VMEM((positions, channels), BF16),
            pltpu.VMEM((positions, channels), BF16),
            pltpu.SemaphoreType.DMA((10,)),
        ],
        compiler_params=PARAMS,
        name="block_backward",
    )
    made = blank((*kept, one, *saved, one))
    stash, received = tuple(made[: len(kept)]), made[len(kept)]
    grads, returned = tuple(made[len(kept) + 1 : -1]), made[-1]
    route = [(i, i + 1) for i in range(sections - 1)]
    back_route = [(i + 1, i) for i in range(sections - 1)]
    ticks = micro + sections - 1

    def forward_tick(tick, received, stash):
        slot = tick - section
        active = (slot >= 0) & (slot < micro)
        slot = jnp.clip(slot, 0, micro - 1)
        sc = jnp.stack(
            [active.astype(jnp.int32), (section == 0).astype(jnp.int32), slot, roster[0, slot]]
        )
        *stash, y = forward_call(
            sc, received, images, taps, layer_scale, up, down, *stash
        )
        return tuple(stash), y

    def forward_loop(tick, state):
        received, stash = state
        stash, y = forward_tick(tick, received, stash)
        return lax.ppermute(y, "section", route), stash

    received, stash = lax.fori_loop(0, ticks - 1, forward_loop, (received, stash))
    stash, _ = forward_tick(ticks - 1, received, stash)
    outputs, x_s, n_s, istd_s, hid_s, slope_s, branch_s = stash

    def backward_tick(tick, returned, grads):
        slot = tick - (sections - 1 - section)
        active = (slot >= 0) & (slot < micro)
        slot = jnp.clip(slot, 0, micro - 1)
        sc = jnp.stack(
            [
                active.astype(jnp.int32),
                (section == sections - 1).astype(jnp.int32),
                slot,
                (section > 0).astype(jnp.int32),
            ]
        )
        *grads, g = backward_call(
            sc, returned, cotangent, taps, layer_scale, up, down, n_s, istd_s, slope_s, *grads
        )
        return tuple(grads), g

    def backward_loop(tick, state):
        returned, grads = state
        grads, g = backward_tick(tick, returned, grads)
        return lax.ppermute(g, "section", back_route), grads

    returned, grads = lax.fori_loop(0, ticks - 1, backward_loop, (returned, grads))
    grads, _ = backward_tick(ticks - 1, returned, grads)
    go_s, gp_s, gc_s = grads

    real_rows = (side * side * channels + 2 * channels * width + channels) // LANES
    slot_count = master.shape[1]
    share = -(-slot_count // 16) * 16
    buckets = bucket_owner.shape[1]
    slots = pl.pallas_call(
        functools.partial(weight_kernel, (*dims, real_rows, replicas, buckets)),
        out_shape=sds((replicas, share, LANES), BF16),
        in_specs=[SMEM, SMEM, VMEM] + [ANY] * 7,
        out_specs=ANY,
        scratch_shapes=[
            pltpu.VMEM((micro * positions, channels), BF16),
            pltpu.VMEM((micro * positions, channels), BF16),
            pltpu.VMEM((micro * positions, width), BF16),
            pltpu.VMEM((micro * positions, channels), F32),
            pltpu.VMEM((micro * positions, channels), BF16),
            pltpu.VMEM((micro * positions, width), BF16),
            pltpu.VMEM((micro * positions, channels), BF16),
            pltpu.VMEM((micro * positions, channels), BF16),
            pltpu.VMEM(pad_shape, F32),
            pltpu.VMEM((-(-real_rows // replicas) * replicas + STEP, LANES), F32),
            pltpu.VMEM((share + 2 * STEP, LANES), F32),
            pltpu.VMEM((2, share, LANES), BF16),
            pltpu.SMEM((buckets,), jnp.int32),
            pltpu.SMEM((buckets,), jnp.int32),
            pltpu.SMEM((replicas,), jnp.int32),
            pltpu.SemaphoreType.DMA((7 * micro + 2,)),
        ],
        compiler_params=PARAMS,
        name="weight_grads",
    )(
        bucket_bounds[0], bucket_owner[0], layer_scale, x_s, n_s, hid_s, branch_s, go_s, gp_s, gc_s
    )
    summed = lax.psum_scatter(slots, "dp", scatter_dimension=0, tiled=False)
    quads = slot_count // 4
    count = 67 if quads % 67 == 0 else 1
    part = pl.BlockSpec((count, 4, LANES), lambda i: (i, 0, 0))
    quad = sds((quads, 4, LANES), F32)
    new = pl.pallas_call(
        functools.partial(adam_kernel, count, replicas),
        grid=(quads // count,),
        out_shape=(quad, quad, quad),
        in_specs=[pl.BlockSpec((share, LANES), lambda i: (0, 0)), part, part, part],
        out_specs=[part, part, part],
        scratch_shapes=[pltpu.VMEM((share, LANES), F32)],
        compiler_params=PARAMS,
        name="adam",
    )(
        summed,
        master.reshape(quads, 4, LANES),
        first_moment.reshape(quads, 4, LANES),
        second_moment.reshape(quads, 4, LANES),
    )
    new_master, new_first, new_second = (value.reshape(master.shape) for value in new)
    return (
        outputs.reshape(1, micro, height, breadth, channels),
        new_master,
        new_first,
        new_second,
    )


def solution(mesh):
    placed = (
        P("dp", None, None, None),
        P("dp", None),
        P("dp", None, None, None),
        P("section", None, None, None),
        P("section", None, None),
        P("section", None, None),
        P("section", None),
        P("section", "dp", None),
        P("section", "dp", None),
        P("section", "dp", None),
        P("section", None),
        P("section", None),
    )
    return jax.shard_map(
        body,
        mesh=mesh,
        in_specs=placed,
        out_specs=(
            P("section", "dp", None, None, None),
            P("section", "dp", None),
            P("section", "dp", None),
            P("section", "dp", None),
        ),
        check_vma=False,
    )
```

```python
import functools

import jax
import jax.numpy as jnp
from jax import lax
from jax.experimental import pallas as pl
from jax.experimental.pallas import tpu as pltpu
from jax.sharding import PartitionSpec as P

beta_one = 0.9
beta_two = 0.95
learn_rate = 0.01
decay_rate = 0.1
adam_eps = 1e-08
norm_eps = 1e-06
first_fix = 1.0 - 0.9**10
second_fix = 1.0 - 0.95**10

LANES = 128
MARGIN = 8
STEP = 64
F32 = jnp.float32
BF16 = jnp.bfloat16
ANY = pl.BlockSpec(memory_space=pl.ANY)
SMEM = pl.BlockSpec(memory_space=pltpu.SMEM)
VMEM = pl.BlockSpec(memory_space=pltpu.VMEM)
PARAMS = pltpu.CompilerParams(vmem_limit_bytes=56 * 1024 * 1024)


def rolled(count):
    def wrap(fn):
        lax.fori_loop(0, count, lambda i, c: (fn(i), c)[1], 0)

    return wrap


def pad_map(pad, image, reach, height, breadth):
    chunks = pad.shape[0]
    for c in range(chunks):
        for r in range(pad.shape[1]):
            if r < reach or r >= reach + height:
                pad[c, r] = jnp.zeros(pad.shape[2:], F32)
            else:
                pad[c, r, :MARGIN] = jnp.zeros((MARGIN, LANES), F32)
                pad[c, r, MARGIN + breadth :] = jnp.zeros((MARGIN, LANES), F32)
                pad[c, r, MARGIN : MARGIN + breadth] = image[
                    (r - reach) * breadth : (r - reach + 1) * breadth,
                    c * LANES : (c + 1) * LANES,
                ].astype(F32)


def depthwise(pad, taps, result, side, height, breadth, flip):
    reach = (side - 1) // 2
    halves = breadth // 8

    @rolled(pad.shape[0])
    def _(c):
        sums = [[None] * halves for _ in range(height)]
        for b in range(side):
            weights = []
            for a in range(side):
                t = a * side + b
                t = side * side - 1 - t if flip else t
                weights.append(jnp.broadcast_to(taps[c, pl.ds(t, 1), :], (8, LANES)))
            for r in range(height + 2 * reach):
                for w in range(halves):
                    value = pad[c, r, pl.ds(MARGIN - reach + b + 8 * w, 8), :]
                    for a in range(side):
                        i = r - a
                        if 0 <= i < height:
                            term = value * weights[a]
                            sums[i][w] = term if sums[i][w] is None else sums[i][w] + term
        columns = pl.ds(pl.multiple_of(c * LANES, LANES), LANES)
        for i in range(height):
            for w in range(halves):
                result[pl.ds(i * breadth + 8 * w, 8), columns] = sums[i][w]


def forward_kernel(
    dims, tick, place, roster, xr, images, taps, scale, up, down, *refs
):
    side, height, breadth, width = dims
    out_o, x_o, n_o, istd_o, hid_o, slope_o, branch_o, y = refs[7:15]
    xv, pad, conv, nv, iv, upv, downv, hv, sv, acc, yv, sems = refs[15:]
    positions, channels = xv.shape
    micro = images.shape[0]
    reach = (side - 1) // 2
    slot = tick[0] - place[0]

    @pl.when((slot >= 0) & (slot < micro))
    def _():
        up_in = pltpu.make_async_copy(up, upv, sems.at[0])
        down_in = pltpu.make_async_copy(down, downv, sems.at[1])

        @pl.when(place[0] == 0)
        def _():
            cp = pltpu.make_async_copy(images.at[roster[0, slot]], xv, sems.at[2])
            cp.start()
            up_in.start()
            down_in.start()
            cp.wait()

        @pl.when(place[0] > 0)
        def _():
            cp = pltpu.make_async_copy(xr, xv, sems.at[2])
            cp.start()
            up_in.start()
            down_in.start()
            cp.wait()

        x_out = pltpu.make_async_copy(xv, x_o.at[slot], sems.at[3])
        x_out.start()
        pad_map(pad, xv, reach, height, breadth)
        depthwise(pad, taps, conv, side, height, breadth, False)
        block = 64
        for p in range(0, positions, block):
            rows = conv[p : p + block, :]
            centred = rows - jnp.mean(rows, axis=-1, keepdims=True)
            inv_std = lax.rsqrt(jnp.mean(centred * centred, axis=-1, keepdims=True) + norm_eps)
            nv[p : p + block, :] = (centred * inv_std).astype(BF16)
            iv[p : p + block, :] = jnp.broadcast_to(inv_std, (block, LANES))
        n_out = pltpu.make_async_copy(nv, n_o.at[slot], sems.at[4])
        n_out.start()
        i_out = pltpu.make_async_copy(iv, istd_o.at[slot], sems.at[5])
        i_out.start()
        up_in.wait()
        down_in.wait()
        step = 512
        for k in range(0, width, step):
            pre = jnp.dot(nv[...], upv[:, k : k + step], preferred_element_type=F32)
            cdf = 0.5 * (1.0 + lax.erf(pre * 0.7071067811865476))
            hidden = (pre * cdf).astype(BF16)
            hv[:, k : k + step] = hidden
            bell = jnp.exp(-0.5 * pre * pre) * 0.3989422804014327
            sv[:, k : k + step] = (cdf + pre * bell).astype(BF16)
            part = jnp.dot(hidden, downv[k : k + step, :], preferred_element_type=F32)
            if k == 0:
                acc[...] = part
            else:
                acc[...] += part
        yv[...] = (xv[...].astype(F32) + scale[...] * acc[...]).astype(BF16)
        y_out = pltpu.make_async_copy(yv, y, sems.at[6])
        y_out.start()
        o_out = pltpu.make_async_copy(yv, out_o.at[slot], sems.at[7])
        o_out.start()
        h_out = pltpu.make_async_copy(hv, hid_o.at[slot], sems.at[8])
        h_out.start()
        s_out = pltpu.make_async_copy(sv, slope_o.at[slot], sems.at[9])
        s_out.start()
        b_out = pltpu.make_async_copy(acc, branch_o.at[slot], sems.at[10])
        b_out.start()
        for cp in (x_out, n_out, i_out, y_out, o_out, h_out, s_out, b_out):
            cp.wait()


def backward_kernel(
    dims, tick, place, gr, cotangent, taps, scale, up, down, n_i, istd_i, slope_i, *refs
):
    side, height, breadth, width = dims
    go_o, gp_o, gc_o, g_in = refs[3:7]
    gv, pad, conv, nv, iv, upv, downv, sv, gpv, acc, scaled, gcv, yv, sems = refs[7:]
    positions, channels = gv.shape
    micro = cotangent.shape[0]
    reach = (side - 1) // 2
    slot = tick[0] - place[1]

    @pl.when((slot >= 0) & (slot < micro))
    def _():
        down_in = pltpu.make_async_copy(down, downv, sems.at[0])
        up_in = pltpu.make_async_copy(up, upv, sems.at[1])
        s_in = pltpu.make_async_copy(slope_i.at[slot], sv, sems.at[3])
        n_in = pltpu.make_async_copy(n_i.at[slot], nv, sems.at[4])
        i_in = pltpu.make_async_copy(istd_i.at[slot], iv, sems.at[5])

        def begin(source):
            cp = pltpu.make_async_copy(source, gv, sems.at[2])
            cp.start()
            down_in.start()
            s_in.start()
            up_in.start()
            n_in.start()
            i_in.start()
            cp.wait()

        @pl.when(place[1] == 0)
        def _():
            begin(cotangent.at[slot])

        @pl.when(place[1] > 0)
        def _():
            begin(gr)

        go_out = pltpu.make_async_copy(gv, go_o.at[slot], sems.at[6])
        go_out.start()
        scaled[...] = (gv[...].astype(F32) * scale[...]).astype(BF16)
        down_in.wait()
        s_in.wait()
        up_in.wait()
        step = 512
        across = (((1,), (1,)), ((), ()))
        for k in range(0, width, step):
            grad_hidden = lax.dot_general(
                scaled[...], downv[k : k + step, :], across, preferred_element_type=F32
            )
            grad_pre = (grad_hidden * sv[:, k : k + step].astype(F32)).astype(BF16)
            gpv[:, k : k + step] = grad_pre
            part = lax.dot_general(
                grad_pre, upv[:, k : k + step], across, preferred_element_type=F32
            )
            if k == 0:
                acc[...] = part
            else:
                acc[...] += part
        gp_out = pltpu.make_async_copy(gpv, gp_o.at[slot], sems.at[7])
        gp_out.start()
        n_in.wait()
        i_in.wait()
        block = 64
        for p in range(0, positions, block):
            rows = acc[p : p + block, :]
            normed = nv[p : p + block, :].astype(F32)
            mean = jnp.mean(rows, axis=-1, keepdims=True)
            slant = jnp.mean(rows * normed, axis=-1, keepdims=True)
            gcv[p : p + block, :] = (
                iv[p : p + block, :1] * (rows - mean - normed * slant)
            ).astype(BF16)
        gc_out = pltpu.make_async_copy(gcv, gc_o.at[slot], sems.at[8])
        gc_out.start()

        @pl.when(place[0] > 0)
        def _():
            pad_map(pad, gcv, reach, height, breadth)
            depthwise(pad, taps, conv, side, height, breadth, True)
            yv[...] = (gv[...].astype(F32) + conv[...]).astype(BF16)
            cp = pltpu.make_async_copy(yv, g_in, sems.at[9])
            cp.start()
            cp.wait()

        for cp in (go_out, gp_out, gc_out):
            cp.wait()


def weight_kernel(
    dims, bounds, owners, order, scale, x_i, n_i, hid_i, branch_i, go_i, gp_i, gc_i, *refs
):
    side, height, breadth, width, real_rows, owner_count, buckets, share, cut = dims
    pieces, refs = refs[:PIECES], refs[PIECES:]
    (xv, nv, hv, bv, gv, gpv, gcv, scaled, pad, flat, stage, ready, starts, lengths, counts, sems) = refs
    micro, positions, channels = x_i.shape
    reach = (side - 1) // 2
    chunks = channels // LANES
    rows = micro * positions
    tap_rows = side * side * chunks
    up_rows = channels * (width // LANES)
    down_base = tap_rows + up_rows
    scale_base = down_base + up_rows
    copies = []
    for q, (src, dst) in enumerate(
        ((n_i, nv), (gp_i, gpv), (go_i, gv), (hid_i, hv), (x_i, xv), (gc_i, gcv), (branch_i, bv))
    ):
        for m in range(micro):
            cp = pltpu.make_async_copy(
                src.at[m], dst.at[pl.ds(m * positions, positions)], sems.at[q * micro + m]
            )
            cp.start()
            copies.append(cp)
    for d in range(owner_count):
        counts[d] = 0

    @rolled(buckets)
    def _(b):
        d = owners[b]
        at = d * (buckets // owner_count) + counts[d]
        starts[at] = bounds[b]
        lengths[at] = bounds[b + 1] - bounds[b]
        counts[d] = counts[d] + 1

    for cp in copies:
        cp.wait()
    along = (((0,), (0,)), ((), ()))
    scaled[...] = (gv[...].astype(F32) * scale[...]).astype(BF16)
    for j in range(0, width // LANES, 2):
        part = lax.dot_general(
            nv[...], gpv[:, j * LANES : (j + 2) * LANES], along, preferred_element_type=F32
        )
        for q in range(2):
            flat[pl.ds(tap_rows + j + q, channels, stride=width // LANES), :] = part[
                :, q * LANES : (q + 1) * LANES
            ]
    for j in range(0, chunks, 2):
        part = lax.dot_general(
            hv[...], scaled[:, j * LANES : (j + 2) * LANES], along, preferred_element_type=F32
        )
        for q in range(2):
            flat[pl.ds(down_base + j + q, width, stride=chunks), :] = part[
                :, q * LANES : (q + 1) * LANES
            ]
    terms = jnp.sum(gv[...].astype(F32) * bv[...], axis=0, keepdims=True)
    for c in range(chunks):
        flat[pl.ds(scale_base + c, 1), :] = terms[:, c * LANES : (c + 1) * LANES]
    tail = flat.shape[0] - scale_base - chunks
    flat[pl.ds(scale_base + chunks, tail), :] = jnp.zeros((tail, LANES), F32)
    halves = breadth // 8
    for m in range(micro):
        pad_map(pad, xv.at[pl.ds(m * positions, positions)], reach, height, breadth)

        @rolled(chunks)
        def _(c):
            columns = pl.ds(pl.multiple_of(c * LANES, LANES), LANES)
            grads = [
                gcv[pl.ds(m * positions + 16 * i, 16), columns].astype(F32)
                for i in range(positions // 16)
            ]
            for b in range(side):
                sums = [None] * side
                for r in range(reach, height + reach):
                    for w in range(halves):
                        value = pad[c, r, pl.ds(MARGIN - reach + b + 8 * w, 8), :]
                        for a in range(side):
                            i = r - a
                            if 0 <= i < height:
                                p = i * breadth + 8 * w
                                term = value * grads[p // 16][p % 16 : p % 16 + 8]
                                sums[a] = term if sums[a] is None else sums[a] + term
                for a in range(side):
                    total = jnp.sum(sums[a], axis=0, keepdims=True)
                    at = pl.ds((a * side + b) * chunks + c, 1)
                    if m == 0:
                        flat[at, :] = total
                    else:
                        flat[at, :] += total

    half = (share - cut) // 2
    spans = ((0, cut), (cut, half), (cut + half, half))

    def out_copies(target, q, n):
        result = []
        for part, (first, size) in enumerate(spans):
            piece, at = target[part]
            result.append(
                pltpu.make_async_copy(
                    ready.at[q, pl.ds(first, size)],
                    pieces[piece].at[at],
                    sems.at[7 * micro + 3 * q + part],
                )
            )
        return result

    waiting = [None, None]
    for n, target in enumerate(relay_targets()):
        q = n % 2
        d = order[n]
        offset = 0
        for k in range(buckets // owner_count):
            at = d * (buckets // owner_count) + k
            start, length = starts[at], lengths[at]
            here = offset

            def move(i, c, start=start, here=here):
                stage[pl.ds(here + STEP * i, STEP), :] = flat[pl.ds(start + STEP * i, STEP), :]
                return c

            lax.fori_loop(0, lax.div(length + STEP - 1, STEP), move, 0)
            offset = offset + length

        def clear(i, c, offset=offset):
            stage[pl.ds(offset + STEP * i, STEP), :] = jnp.zeros((STEP, LANES), F32)
            return c

        lax.fori_loop(0, lax.div(share - offset + STEP - 1, STEP), clear, 0)
        if waiting[q] is not None:
            for cp in waiting[q]:
                cp.wait()
        ready[q] = stage[:share, :].astype(BF16)
        waiting[q] = out_copies(target, q, n)
        for cp in waiting[q]:
            cp.start()
    for q in range(2):
        for cp in waiting[q]:
            cp.wait()


ORBIT = 4
PIECES = 12


def relay_order():
    order = []
    for core in (1, 0):
        for z, x in ((0, 3), (1, 1), (0, 2), (1, 2), (0, 1), (1, 3), (0, 0), (1, 0)):
            order.append((core, z, x))
    return order


def relay_targets():
    turn = {(0, 3): 0, (1, 1): 0, (0, 2): 1, (1, 2): 1, (0, 1): 2, (1, 3): 2, (0, 0): 3, (1, 0): 3}
    result = []
    for core, z, x in relay_order():
        base = 6 * (1 - core)
        q = base + 4 + (1 - z)
        result.append(((base + turn[z, x], z), (q, x), (q, ORBIT + x)))
    return result


def piece_shapes(share, cut):
    half = (share - cut) // 2
    one = [(2, cut, LANES)] * 4 + [(2 * ORBIT, half, LANES)] * 2
    return one + one


def owner_order(me):
    z, x, core = me // 8, (me // 2) % 4, me % 2
    return jnp.stack(
        [((z + dz) % 2) * 8 + ((x + dx) % 4) * 2 + (core + dc) % 2 for dc, dz, dx in relay_order()]
    ).astype(jnp.int32)


def routes():
    def route(to):
        pairs = []
        for me in range(16):
            z, x, core = me // 8, (me // 2) % 4, me % 2
            z, x, core = to(z, x, core)
            pairs.append((me, z * 8 + x * 2 + core))
        return pairs

    return (
        route(lambda z, x, c: (z, x, 1 - c)),
        route(lambda z, x, c: (z, (x + 1) % 4, c)),
        route(lambda z, x, c: (z, (x + 3) % 4, c)),
        route(lambda z, x, c: (1 - z, x, c)),
    )


def plus(*values):
    total = values[0].astype(F32)
    for value in values[1:]:
        total = total + value.astype(F32)
    return total.astype(BF16)


def relay_sum(pieces):
    across, right, left, over = routes()
    sent, kept = pieces[:6], pieces[6:]
    half = sent[4].shape[1]

    def hop(value, route):
        return lax.ppermute(value, "dp", route)

    came = [None] * 6
    for q in (0, 4, 1, 2, 5, 3):
        came[q] = hop(sent[q], across)
    r = hop(plus(kept[0][0], came[0][0]), right)
    l = hop(plus(kept[0][1], came[0][1]), left)
    far = hop(plus(kept[4][:ORBIT], came[4][:ORBIT]), over)
    farther = hop(plus(kept[4][ORBIT:], came[4][ORBIT:]), over)
    for q in (1, 2):
        r = hop(plus(kept[q][0], came[q][0], r), right)
        l = hop(plus(kept[q][1], came[q][1], l), left)
    z_sent = hop(plus(kept[3][1], came[3][1], l), over)
    near = (kept[5][:ORBIT], came[5][:ORBIT], far)
    nearer = (kept[5][ORBIT:], came[5][ORBIT:], farther)
    a = hop(plus(*(v[3] for v in near)), right)
    b = hop(plus(*(v[1] for v in nearer)), left)
    for step in (2, 1):
        a = hop(plus(*(v[step] for v in near), a), right)
        b = hop(plus(*(v[4 - step] for v in nearer), b), left)
    first = (kept[3][0], came[3][0], r, z_sent)
    return first, tuple(v[0] for v in near) + (a,), tuple(v[0] for v in nearer) + (b,)


def adam_kernel(count, replicas, g_i, m_i, f_i, s_i, m_o, f_o, s_o, grads):
    @pl.when(pl.program_id(0) == 0)
    def _():
        grads[...] = g_i[...].astype(F32) * (1.0 / replicas)

    base = pl.program_id(0) * (4 * count)
    for k in range(count):
        grad = grads[pl.ds(base + 4 * k, 4), :]
        new_first = beta_one * f_i[k] + (1.0 - beta_one) * grad
        new_second = beta_two * s_i[k] + (1.0 - beta_two) * grad * grad
        update = (
            new_first / first_fix / (jnp.sqrt(new_second / second_fix) + adam_eps)
            + decay_rate * m_i[k]
        )
        m_o[k] = m_i[k] - learn_rate * update
        f_o[k] = new_first
        s_o[k] = new_second


def blank(shapes):
    def kernel(*refs):
        pass

    return pl.pallas_call(
        kernel, out_shape=shapes, out_specs=[ANY] * len(shapes), name="blank"
    )()


def body(
    images,
    roster,
    cotangent,
    depth_kernel,
    up_weight,
    down_weight,
    layer_scale,
    master,
    first_moment,
    second_moment,
    bucket_bounds,
    bucket_owner,
):
    sections = lax.axis_size("section")
    replicas = lax.axis_size("dp")
    section = lax.axis_index("section")
    micro, height, breadth, channels = images.shape
    side = depth_kernel.shape[1]
    width = up_weight.shape[2]
    positions = height * breadth
    chunks = channels // LANES
    up, down = up_weight[0], down_weight[0]
    taps = (
        depth_kernel[0].astype(F32).reshape(side * side, chunks, LANES).transpose(1, 0, 2)
    )
    images = images.reshape(micro, positions, channels)
    cotangent = cotangent.reshape(micro, positions, channels)
    sds = jax.ShapeDtypeStruct
    act = sds((micro, positions, channels), BF16)
    wide = sds((micro, positions, width), BF16)
    one = sds((positions, channels), BF16)
    spread = sds((micro, positions, LANES), F32)
    full = sds((micro, positions, channels), F32)
    pad_shape = (chunks, height + side - 1, breadth + 2 * MARGIN, LANES)
    dims = (side, height, breadth, width)

    kept = (act, act, act, spread, wide, wide, full)
    forward_call = pl.pallas_call(
        functools.partial(forward_kernel, dims),
        out_shape=(*kept, one),
        in_specs=[SMEM, SMEM, SMEM, ANY, ANY, VMEM, VMEM, ANY, ANY] + [ANY] * len(kept),
        out_specs=[ANY] * (len(kept) + 1),
        input_output_aliases={9 + q: q for q in range(len(kept))},
        scratch_shapes=[
            pltpu.VMEM((positions, channels), BF16),
            pltpu.VMEM(pad_shape, F32),
            pltpu.VMEM((positions, channels), F32),
            pltpu.VMEM((positions, channels), BF16),
            pltpu.VMEM((positions, LANES), F32),
            pltpu.VMEM((channels, width), BF16),
            pltpu.VMEM((width, channels), BF16),
            pltpu.VMEM((positions, width), BF16),
            pltpu.VMEM((positions, width), BF16),
            pltpu.VMEM((positions, channels), F32),
            pltpu.VMEM((positions, channels), BF16),
            pltpu.SemaphoreType.DMA((11,)),
        ],
        compiler_params=PARAMS,
        name="block_forward",
    )
    saved = (act, wide, act)
    backward_call = pl.pallas_call(
        functools.partial(backward_kernel, dims),
        out_shape=(*saved, one),
        in_specs=[SMEM, SMEM, ANY, ANY, VMEM, VMEM, ANY, ANY, ANY, ANY, ANY] + [ANY] * len(saved),
        out_specs=[ANY] * (len(saved) + 1),
        input_output_aliases={11 + q: q for q in range(len(saved))},
        scratch_shapes=[
            pltpu.VMEM((positions, channels), BF16),
            pltpu.VMEM(pad_shape, F32),
            pltpu.VMEM((positions, channels), F32),
            pltpu.VMEM((positions, channels), BF16),
            pltpu.VMEM((positions, LANES), F32),
            pltpu.VMEM((channels, width), BF16),
            pltpu.VMEM((width, channels), BF16),
            pltpu.VMEM((positions, width), BF16),
            pltpu.VMEM((positions, width), BF16),
            pltpu.VMEM((positions, channels), F32),
            pltpu.VMEM((positions, channels), BF16),
            pltpu.VMEM((positions, channels), BF16),
            pltpu.VMEM((positions, channels), BF16),
            pltpu.SemaphoreType.DMA((10,)),
        ],
        compiler_params=PARAMS,
        name="block_backward",
    )
    made = blank((*kept, one, *saved, one))
    stash, received = tuple(made[: len(kept)]), made[len(kept)]
    grads, returned = tuple(made[len(kept) + 1 : -1]), made[-1]
    route = [(i, i + 1) for i in range(sections - 1)]
    back_route = [(i + 1, i) for i in range(sections - 1)]
    ticks = micro + sections - 1
    order = owner_order(lax.axis_index("dp"))
    place = jnp.stack([section, sections - 1 - section]).astype(jnp.int32)

    def forward_tick(tick, received, stash):
        *stash, y = forward_call(
            tick.reshape(1), place, roster, received, images, taps, layer_scale, up, down, *stash
        )
        return tuple(stash), y

    def forward_loop(tick, state):
        received, stash = state
        stash, y = forward_tick(tick, received, stash)
        return lax.ppermute(y, "section", route), stash

    received, stash = lax.fori_loop(0, ticks - 1, forward_loop, (received, stash))
    stash, _ = forward_tick(jnp.int32(ticks - 1), received, stash)
    outputs, x_s, n_s, istd_s, hid_s, slope_s, branch_s = stash

    def backward_tick(tick, returned, grads):
        *grads, g = backward_call(
            tick.reshape(1), place, returned, cotangent, taps, layer_scale, up, down, n_s, istd_s, slope_s, *grads
        )
        return tuple(grads), g

    def backward_loop(tick, state):
        returned, grads = state
        grads, g = backward_tick(tick, returned, grads)
        return lax.ppermute(g, "section", back_route), grads

    returned, grads = lax.fori_loop(0, ticks - 1, backward_loop, (returned, grads))
    grads, _ = backward_tick(jnp.int32(ticks - 1), returned, grads)
    go_s, gp_s, gc_s = grads

    real_rows = (side * side * channels + 2 * channels * width + channels) // LANES
    slot_count = master.shape[1]
    share = -(-slot_count // 16) * 16
    buckets = bucket_owner.shape[1]
    cut = share * 4 // 7 // 32 * 32 + share % 32
    pieces = pl.pallas_call(
        functools.partial(
            weight_kernel, (*dims, real_rows, replicas, buckets, share, cut)
        ),
        out_shape=tuple(sds(shape, BF16) for shape in piece_shapes(share, cut)),
        in_specs=[SMEM, SMEM, SMEM, VMEM] + [ANY] * 7,
        out_specs=[ANY] * PIECES,
        scratch_shapes=[
            pltpu.VMEM((micro * positions, channels), BF16),
            pltpu.VMEM((micro * positions, channels), BF16),
            pltpu.VMEM((micro * positions, width), BF16),
            pltpu.VMEM((micro * positions, channels), F32),
            pltpu.VMEM((micro * positions, channels), BF16),
            pltpu.VMEM((micro * positions, width), BF16),
            pltpu.VMEM((micro * positions, channels), BF16),
            pltpu.VMEM((micro * positions, channels), BF16),
            pltpu.VMEM(pad_shape, F32),
            pltpu.VMEM((-(-real_rows // replicas) * replicas + STEP, LANES), F32),
            pltpu.VMEM((share + 2 * STEP, LANES), F32),
            pltpu.VMEM((2, share, LANES), BF16),
            pltpu.SMEM((buckets,), jnp.int32),
            pltpu.SMEM((buckets,), jnp.int32),
            pltpu.SMEM((replicas,), jnp.int32),
            pltpu.SemaphoreType.DMA((7 * micro + 6,)),
        ],
        compiler_params=PARAMS,
        name="weight_grads",
    )(
        bucket_bounds[0], bucket_owner[0], order, layer_scale, x_s, n_s, hid_s, branch_s, go_s, gp_s, gc_s
    )
    summed = jnp.concatenate([plus(*values) for values in relay_sum(pieces)])
    quads = slot_count // 4
    count = 67 if quads % 67 == 0 else 1
    part = pl.BlockSpec((count, 4, LANES), lambda i: (i, 0, 0))
    quad = sds((quads, 4, LANES), F32)
    new = pl.pallas_call(
        functools.partial(adam_kernel, count, replicas),
        grid=(quads // count,),
        out_shape=(quad, quad, quad),
        in_specs=[pl.BlockSpec((share, LANES), lambda i: (0, 0)), part, part, part],
        out_specs=[part, part, part],
        scratch_shapes=[pltpu.VMEM((share, LANES), F32)],
        compiler_params=PARAMS,
        name="adam",
    )(
        summed,
        master.reshape(quads, 4, LANES),
        first_moment.reshape(quads, 4, LANES),
        second_moment.reshape(quads, 4, LANES),
    )
    new_master, new_first, new_second = (value.reshape(master.shape) for value in new)
    return (
        outputs.reshape(1, micro, height, breadth, channels),
        new_master,
        new_first,
        new_second,
    )


def solution(mesh):
    placed = (
        P("dp", None, None, None),
        P("dp", None),
        P("dp", None, None, None),
        P("section", None, None, None),
        P("section", None, None),
        P("section", None, None),
        P("section", None),
        P("section", "dp", None),
        P("section", "dp", None),
        P("section", "dp", None),
        P("section", None),
        P("section", None),
    )
    return jax.shard_map(
        body,
        mesh=mesh,
        in_specs=placed,
        out_specs=(
            P("section", "dp", None, None, None),
            P("section", "dp", None),
            P("section", "dp", None),
            P("section", "dp", None),
        ),
        check_vma=False,
    )
```

```python
import functools

import jax
import jax.numpy as jnp
from jax import lax
from jax.experimental import pallas as pl
from jax.experimental.pallas import tpu as pltpu
from jax.sharding import PartitionSpec as P

beta_one = 0.9
beta_two = 0.95
learn_rate = 0.01
decay_rate = 0.1
adam_eps = 1e-08
norm_eps = 1e-06
first_fix = 1.0 - 0.9**10
second_fix = 1.0 - 0.95**10

LANES = 128
MARGIN = 8
STEP = 64
SLICE = 512
F32 = jnp.float32
BF16 = jnp.bfloat16
ANY = pl.BlockSpec(memory_space=pl.ANY)
SMEM = pl.BlockSpec(memory_space=pltpu.SMEM)
VMEM = pl.BlockSpec(memory_space=pltpu.VMEM)
PARAMS = pltpu.CompilerParams(vmem_limit_bytes=56 * 1024 * 1024)


def rolled(count):
    def wrap(fn):
        lax.fori_loop(0, count, lambda i, c: (fn(i), c)[1], 0)

    return wrap


def pad_map(pad, image, reach, height, breadth):
    chunks = pad.shape[0]
    for c in range(chunks):
        for r in range(pad.shape[1]):
            if r < reach or r >= reach + height:
                pad[c, r] = jnp.zeros(pad.shape[2:], F32)
            else:
                pad[c, r, :MARGIN] = jnp.zeros((MARGIN, LANES), F32)
                pad[c, r, MARGIN + breadth :] = jnp.zeros((MARGIN, LANES), F32)
                pad[c, r, MARGIN : MARGIN + breadth] = image[
                    (r - reach) * breadth : (r - reach + 1) * breadth,
                    c * LANES : (c + 1) * LANES,
                ].astype(F32)


def depthwise(pad, taps, result, side, height, breadth, flip):
    reach = (side - 1) // 2
    halves = breadth // 8

    @rolled(pad.shape[0])
    def _(c):
        sums = [[None] * halves for _ in range(height)]
        for b in range(side):
            weights = []
            for a in range(side):
                t = a * side + b
                t = side * side - 1 - t if flip else t
                weights.append(jnp.broadcast_to(taps[c, pl.ds(t, 1), :], (8, LANES)))
            for r in range(height + 2 * reach):
                for w in range(halves):
                    value = pad[c, r, pl.ds(MARGIN - reach + b + 8 * w, 8), :]
                    for a in range(side):
                        i = r - a
                        if 0 <= i < height:
                            term = value * weights[a]
                            sums[i][w] = term if sums[i][w] is None else sums[i][w] + term
        columns = pl.ds(pl.multiple_of(c * LANES, LANES), LANES)
        for i in range(height):
            for w in range(halves):
                result[pl.ds(i * breadth + 8 * w, 8), columns] = sums[i][w]


class Streamed:
    def __init__(self, up, upv, down, downv, slope, slopev, sems):
        half = up.shape[1] // 2
        self.parts = []
        for q in range(2):
            cut = pl.ds(q * half, half)
            self.parts.append(
                (
                    pltpu.make_async_copy(down.at[cut], downv.at[cut], sems.at[3 * q]),
                    pltpu.make_async_copy(slope.at[:, cut], slopev.at[:, cut], sems.at[3 * q + 1]),
                    pltpu.make_async_copy(up.at[:, cut], upv.at[:, cut], sems.at[3 * q + 2]),
                )
            )

    def start(self):
        for part in self.parts:
            for cp in part:
                cp.start()

    def wait(self, q):
        for cp in self.parts[q]:
            cp.wait()


def forward_kernel(
    dims, tick, place, roster, xr, images, taps, scale, up, down, *refs
):
    side, height, breadth, width = dims
    out_o, x_o, n_o, istd_o, hid_o, slope_o, branch_o, y = refs[7:15]
    xv, pad, conv, nv, iv, upv, downv, hv, sv, acc, bv, yv, sems = refs[15:]
    positions, channels = xv.shape
    micro = images.shape[0]
    reach = (side - 1) // 2
    slot = tick[0] - place[0]

    @pl.when((slot >= 0) & (slot < micro))
    def _():
        up_in = pltpu.make_async_copy(up, upv, sems.at[0])
        down_in = pltpu.make_async_copy(down, downv, sems.at[1])

        @pl.when(place[0] == 0)
        def _():
            cp = pltpu.make_async_copy(images.at[roster[0, slot]], xv, sems.at[2])
            cp.start()
            up_in.start()
            down_in.start()
            cp.wait()

        @pl.when(place[0] > 0)
        def _():
            cp = pltpu.make_async_copy(xr, xv, sems.at[2])
            cp.start()
            up_in.start()
            down_in.start()
            cp.wait()

        x_out = pltpu.make_async_copy(xv, x_o.at[slot], sems.at[3])
        x_out.start()
        pad_map(pad, xv, reach, height, breadth)
        depthwise(pad, taps, conv, side, height, breadth, False)
        block = 64
        for p in range(0, positions, block):
            rows = conv[p : p + block, :]
            centred = rows - jnp.mean(rows, axis=-1, keepdims=True)
            inv_std = lax.rsqrt(jnp.mean(centred * centred, axis=-1, keepdims=True) + norm_eps)
            nv[p : p + block, :] = (centred * inv_std).astype(BF16)
            iv[p : p + block, :] = jnp.broadcast_to(inv_std, (block, LANES))
        n_out = pltpu.make_async_copy(nv, n_o.at[slot], sems.at[4])
        n_out.start()
        i_out = pltpu.make_async_copy(iv, istd_o.at[slot], sems.at[5])
        i_out.start()
        up_in.wait()
        down_in.wait()
        step = 512
        for k in range(0, width, step):
            pre = jnp.dot(nv[...], upv[:, k : k + step], preferred_element_type=F32)
            cdf = 0.5 * (1.0 + lax.erf(pre * 0.7071067811865476))
            hidden = (pre * cdf).astype(BF16)
            hv[:, k : k + step] = hidden
            bell = jnp.exp(-0.5 * pre * pre) * 0.3989422804014327
            sv[:, k : k + step] = (cdf + pre * bell).astype(BF16)
            part = jnp.dot(hidden, downv[k : k + step, :], preferred_element_type=F32)
            if k == 0:
                acc[...] = part
            else:
                acc[...] += part
        yv[...] = (xv[...].astype(F32) + scale[...] * acc[...]).astype(BF16)
        y_out = pltpu.make_async_copy(yv, y, sems.at[6])
        y_out.start()
        o_out = pltpu.make_async_copy(yv, out_o.at[slot], sems.at[7])
        o_out.start()
        h_out = pltpu.make_async_copy(hv, hid_o.at[slot], sems.at[8])
        h_out.start()
        s_out = pltpu.make_async_copy(sv, slope_o.at[slot], sems.at[9])
        s_out.start()
        bv[...] = acc[...].astype(BF16)
        b_out = pltpu.make_async_copy(bv, branch_o.at[slot], sems.at[10])
        b_out.start()
        for cp in (x_out, n_out, i_out, y_out, o_out, h_out, s_out, b_out):
            cp.wait()


def backward_kernel(
    dims, tick, place, gr, cotangent, taps, scale, up, down, n_i, istd_i, slope_i, *refs
):
    side, height, breadth, width = dims
    go_o, gp_o, gc_o, g_in = refs[3:7]
    gv, pad, conv, nv, iv, upv, downv, sv, gpv, acc, scaled, gcv, yv, sems, weight_sems = refs[7:]
    positions, channels = gv.shape
    micro = cotangent.shape[0]
    reach = (side - 1) // 2
    slot = tick[0] - place[1]

    @pl.when((slot >= 0) & (slot < micro))
    def _():
        weights = Streamed(up, upv, down, downv, slope_i.at[slot], sv, weight_sems)
        n_in = pltpu.make_async_copy(n_i.at[slot], nv, sems.at[4])
        i_in = pltpu.make_async_copy(istd_i.at[slot], iv, sems.at[5])

        def begin(source):
            cp = pltpu.make_async_copy(source, gv, sems.at[2])
            cp.start()
            weights.start()
            n_in.start()
            i_in.start()
            cp.wait()

        @pl.when(place[1] == 0)
        def _():
            begin(cotangent.at[slot])

        @pl.when(place[1] > 0)
        def _():
            begin(gr)

        go_out = pltpu.make_async_copy(gv, go_o.at[slot], sems.at[6])
        go_out.start()
        scaled[...] = (gv[...].astype(F32) * scale[...]).astype(BF16)
        step = SLICE
        across = (((1,), (1,)), ((), ()))
        for k in range(0, width, step):
            if k % (width // 2) == 0:
                weights.wait(k // (width // 2))
            grad_hidden = lax.dot_general(
                scaled[...], downv[k : k + step, :], across, preferred_element_type=F32
            )
            grad_pre = (grad_hidden * sv[:, k : k + step].astype(F32)).astype(BF16)
            gpv[:, k : k + step] = grad_pre
            part = lax.dot_general(
                grad_pre, upv[:, k : k + step], across, preferred_element_type=F32
            )
            if k == 0:
                acc[...] = part
            else:
                acc[...] += part
        gp_out = pltpu.make_async_copy(gpv, gp_o.at[slot], sems.at[7])
        gp_out.start()
        n_in.wait()
        i_in.wait()
        block = 64
        for p in range(0, positions, block):
            rows = acc[p : p + block, :]
            normed = nv[p : p + block, :].astype(F32)
            mean = jnp.mean(rows, axis=-1, keepdims=True)
            slant = jnp.mean(rows * normed, axis=-1, keepdims=True)
            gcv[p : p + block, :] = (
                iv[p : p + block, :1] * (rows - mean - normed * slant)
            ).astype(BF16)
        gc_out = pltpu.make_async_copy(gcv, gc_o.at[slot], sems.at[8])
        gc_out.start()

        @pl.when(place[0] > 0)
        def _():
            pad_map(pad, gcv, reach, height, breadth)
            depthwise(pad, taps, conv, side, height, breadth, True)
            yv[...] = (gv[...].astype(F32) + conv[...]).astype(BF16)
            cp = pltpu.make_async_copy(yv, g_in, sems.at[9])
            cp.start()
            cp.wait()

        for cp in (go_out, gp_out, gc_out):
            cp.wait()


def weight_kernel(
    dims, bounds, owners, order, scale, x_i, n_i, hid_i, branch_i, go_i, gp_i, gc_i, *refs
):
    side, height, breadth, width, real_rows, owner_count, buckets, share, cut = dims
    pieces, refs = refs[:PIECES], refs[PIECES:]
    (xv, nv, hv, bv, gv, gpv, gcv, scaled, pad, flat, stage, ready, starts, lengths, counts, sems) = refs
    micro, positions, channels = x_i.shape
    reach = (side - 1) // 2
    chunks = channels // LANES
    rows = micro * positions
    tap_rows = side * side * chunks
    up_rows = channels * (width // LANES)
    down_base = tap_rows + up_rows
    scale_base = down_base + up_rows
    copies = []
    for q, (src, dst) in enumerate(
        ((x_i, xv), (gc_i, gcv), (n_i, nv), (gp_i, gpv), (go_i, gv), (hid_i, hv), (branch_i, bv))
    ):
        for m in range(micro):
            cp = pltpu.make_async_copy(
                src.at[m], dst.at[pl.ds(m * positions, positions)], sems.at[q * micro + m]
            )
            cp.start()
            copies.append(cp)
    for d in range(owner_count):
        counts[d] = 0

    @rolled(buckets)
    def _(b):
        d = owners[b]
        at = d * (buckets // owner_count) + counts[d]
        starts[at] = bounds[b]
        lengths[at] = bounds[b + 1] - bounds[b]
        counts[d] = counts[d] + 1

    early = 2 * micro
    for cp in copies[:early]:
        cp.wait()
    halves = breadth // 8
    flat[:tap_rows, :] = jnp.zeros((tap_rows, LANES), F32)

    @rolled(micro)
    def _(m):
        base = pl.multiple_of(m * positions, positions)
        pad_map(pad, xv.at[pl.ds(base, positions)], reach, height, breadth)

        @rolled(chunks)
        def _(c):
            columns = pl.ds(pl.multiple_of(c * LANES, LANES), LANES)
            grads = [
                gcv[pl.ds(base + 16 * i, 16), columns].astype(F32)
                for i in range(positions // 16)
            ]
            for b in range(side):
                sums = [None] * side
                for r in range(reach, height + reach):
                    for w in range(halves):
                        value = pad[c, r, pl.ds(MARGIN - reach + b + 8 * w, 8), :]
                        for a in range(side):
                            i = r - a
                            if 0 <= i < height:
                                p = i * breadth + 8 * w
                                term = value * grads[p // 16][p % 16 : p % 16 + 8]
                                sums[a] = term if sums[a] is None else sums[a] + term
                for a in range(side):
                    total = jnp.sum(sums[a], axis=0, keepdims=True)
                    at = pl.ds((a * side + b) * chunks + c, 1)
                    flat[at, :] += total

    for cp in copies[early:]:
        cp.wait()
    along = (((0,), (0,)), ((), ()))
    scaled[...] = (gv[...].astype(F32) * scale[...]).astype(BF16)
    for j in range(0, width // LANES, 2):
        part = lax.dot_general(
            nv[...], gpv[:, j * LANES : (j + 2) * LANES], along, preferred_element_type=F32
        )
        for q in range(2):
            flat[pl.ds(tap_rows + j + q, channels, stride=width // LANES), :] = part[
                :, q * LANES : (q + 1) * LANES
            ]
    for j in range(0, chunks, 2):
        part = lax.dot_general(
            hv[...], scaled[:, j * LANES : (j + 2) * LANES], along, preferred_element_type=F32
        )
        for q in range(2):
            flat[pl.ds(down_base + j + q, width, stride=chunks), :] = part[
                :, q * LANES : (q + 1) * LANES
            ]
    terms = jnp.sum(gv[...].astype(F32) * bv[...].astype(F32), axis=0, keepdims=True)
    for c in range(chunks):
        flat[pl.ds(scale_base + c, 1), :] = terms[:, c * LANES : (c + 1) * LANES]
    tail = flat.shape[0] - scale_base - chunks
    flat[pl.ds(scale_base + chunks, tail), :] = jnp.zeros((tail, LANES), F32)
    half = (share - cut) // 2
    spans = ((0, cut), (cut, half), (cut + half, half))

    def out_copies(target, q, n):
        result = []
        for part, (first, size) in enumerate(spans):
            piece, at = target[part]
            result.append(
                pltpu.make_async_copy(
                    ready.at[q, pl.ds(first, size)],
                    pieces[piece].at[at],
                    sems.at[7 * micro + 3 * q + part],
                )
            )
        return result

    waiting = [None, None]
    for n, target in enumerate(relay_targets()):
        q = n % 2
        d = order[n]
        offset = 0
        for k in range(buckets // owner_count):
            at = d * (buckets // owner_count) + k
            start, length = starts[at], lengths[at]
            here = offset

            def move(i, c, start=start, here=here):
                stage[pl.ds(here + STEP * i, STEP), :] = flat[pl.ds(start + STEP * i, STEP), :]
                return c

            lax.fori_loop(0, lax.div(length + STEP - 1, STEP), move, 0)
            offset = offset + length

        def clear(i, c, offset=offset):
            stage[pl.ds(offset + STEP * i, STEP), :] = jnp.zeros((STEP, LANES), F32)
            return c

        lax.fori_loop(0, lax.div(share - offset + STEP - 1, STEP), clear, 0)
        if waiting[q] is not None:
            for cp in waiting[q]:
                cp.wait()
        ready[q] = stage[:share, :].astype(BF16)
        waiting[q] = out_copies(target, q, n)
        for cp in waiting[q]:
            cp.start()
    for q in range(2):
        for cp in waiting[q]:
            cp.wait()


ORBIT = 4
PIECES = 12


def relay_order():
    order = []
    for core in (1, 0):
        for z, x in ((0, 3), (1, 1), (0, 2), (1, 2), (0, 1), (1, 3), (0, 0), (1, 0)):
            order.append((core, z, x))
    return order


def relay_targets():
    turn = {(0, 3): 0, (1, 1): 0, (0, 2): 1, (1, 2): 1, (0, 1): 2, (1, 3): 2, (0, 0): 3, (1, 0): 3}
    result = []
    for core, z, x in relay_order():
        base = 6 * (1 - core)
        q = base + 4 + (1 - z)
        result.append(((base + turn[z, x], z), (q, x), (q, ORBIT + x)))
    return result


def piece_shapes(share, cut):
    half = (share - cut) // 2
    one = [(2, cut, LANES)] * 4 + [(2 * ORBIT, half, LANES)] * 2
    return one + one


def owner_order(me):
    z, x, core = me // 8, (me // 2) % 4, me % 2
    return jnp.stack(
        [((z + dz) % 2) * 8 + ((x + dx) % 4) * 2 + (core + dc) % 2 for dc, dz, dx in relay_order()]
    ).astype(jnp.int32)


def routes():
    def route(to):
        pairs = []
        for me in range(16):
            z, x, core = me // 8, (me // 2) % 4, me % 2
            z, x, core = to(z, x, core)
            pairs.append((me, z * 8 + x * 2 + core))
        return pairs

    return (
        route(lambda z, x, c: (z, x, 1 - c)),
        route(lambda z, x, c: (z, (x + 1) % 4, c)),
        route(lambda z, x, c: (z, (x + 3) % 4, c)),
        route(lambda z, x, c: (1 - z, x, c)),
    )


def plus(*values):
    total = values[0].astype(F32)
    for value in values[1:]:
        total = total + value.astype(F32)
    return total.astype(BF16)


def relay_sum(pieces):
    across, right, left, over = routes()
    sent, kept = pieces[:6], pieces[6:]
    half = sent[4].shape[1]

    def hop(value, route):
        return lax.ppermute(value, "dp", route)

    came = [None] * 6
    for q in (0, 4, 1, 2, 5, 3):
        came[q] = hop(sent[q], across)
    r = hop(plus(kept[0][0], came[0][0]), right)
    l = hop(plus(kept[0][1], came[0][1]), left)
    far = hop(plus(kept[4][:ORBIT], came[4][:ORBIT]), over)
    farther = hop(plus(kept[4][ORBIT:], came[4][ORBIT:]), over)
    for q in (1, 2):
        r = hop(plus(kept[q][0], came[q][0], r), right)
        l = hop(plus(kept[q][1], came[q][1], l), left)
    z_sent = hop(plus(kept[3][1], came[3][1], l), over)
    near = (kept[5][:ORBIT], came[5][:ORBIT], far)
    nearer = (kept[5][ORBIT:], came[5][ORBIT:], farther)
    a = hop(plus(*(v[3] for v in near)), right)
    b = hop(plus(*(v[1] for v in nearer)), left)
    for step in (2, 1):
        a = hop(plus(*(v[step] for v in near), a), right)
        b = hop(plus(*(v[4 - step] for v in nearer), b), left)
    first = (kept[3][0], came[3][0], r, z_sent)
    return first, tuple(v[0] for v in near) + (a,), tuple(v[0] for v in nearer) + (b,)


def adam_kernel(count, replicas, g_i, m_i, f_i, s_i, m_o, f_o, s_o, grads):
    @pl.when(pl.program_id(0) == 0)
    def _():
        grads[...] = g_i[...].astype(F32) * (1.0 / replicas)

    base = pl.program_id(0) * (4 * count)
    for k in range(count):
        grad = grads[pl.ds(base + 4 * k, 4), :]
        new_first = beta_one * f_i[k] + (1.0 - beta_one) * grad
        new_second = beta_two * s_i[k] + (1.0 - beta_two) * grad * grad
        update = (
            new_first / first_fix / (jnp.sqrt(new_second / second_fix) + adam_eps)
            + decay_rate * m_i[k]
        )
        m_o[k] = m_i[k] - learn_rate * update
        f_o[k] = new_first
        s_o[k] = new_second


def blank(shapes):
    def kernel(*refs):
        pass

    return pl.pallas_call(
        kernel, out_shape=shapes, out_specs=[ANY] * len(shapes), name="blank"
    )()


def body(
    images,
    roster,
    cotangent,
    depth_kernel,
    up_weight,
    down_weight,
    layer_scale,
    master,
    first_moment,
    second_moment,
    bucket_bounds,
    bucket_owner,
):
    sections = lax.axis_size("section")
    replicas = lax.axis_size("dp")
    section = lax.axis_index("section")
    micro, height, breadth, channels = images.shape
    side = depth_kernel.shape[1]
    width = up_weight.shape[2]
    positions = height * breadth
    chunks = channels // LANES
    up, down = up_weight[0], down_weight[0]
    taps = (
        depth_kernel[0].astype(F32).reshape(side * side, chunks, LANES).transpose(1, 0, 2)
    )
    images = images.reshape(micro, positions, channels)
    cotangent = cotangent.reshape(micro, positions, channels)
    sds = jax.ShapeDtypeStruct
    act = sds((micro, positions, channels), BF16)
    wide = sds((micro, positions, width), BF16)
    one = sds((positions, channels), BF16)
    spread = sds((micro, positions, LANES), F32)
    full = sds((micro, positions, channels), BF16)
    pad_shape = (chunks, height + side - 1, breadth + 2 * MARGIN, LANES)
    dims = (side, height, breadth, width)

    kept = (act, act, act, spread, wide, wide, full)
    forward_call = pl.pallas_call(
        functools.partial(forward_kernel, dims),
        out_shape=(*kept, one),
        in_specs=[SMEM, SMEM, SMEM, ANY, ANY, VMEM, VMEM, ANY, ANY] + [ANY] * len(kept),
        out_specs=[ANY] * (len(kept) + 1),
        input_output_aliases={9 + q: q for q in range(len(kept))},
        scratch_shapes=[
            pltpu.VMEM((positions, channels), BF16),
            pltpu.VMEM(pad_shape, F32),
            pltpu.VMEM((positions, channels), F32),
            pltpu.VMEM((positions, channels), BF16),
            pltpu.VMEM((positions, LANES), F32),
            pltpu.VMEM((channels, width), BF16),
            pltpu.VMEM((width, channels), BF16),
            pltpu.VMEM((positions, width), BF16),
            pltpu.VMEM((positions, width), BF16),
            pltpu.VMEM((positions, channels), F32),
            pltpu.VMEM((positions, channels), BF16),
            pltpu.VMEM((positions, channels), BF16),
            pltpu.SemaphoreType.DMA((11,)),
        ],
        compiler_params=PARAMS,
        name="block_forward",
    )
    saved = (act, wide, act)
    backward_call = pl.pallas_call(
        functools.partial(backward_kernel, dims),
        out_shape=(*saved, one),
        in_specs=[SMEM, SMEM, ANY, ANY, VMEM, VMEM, ANY, ANY, ANY, ANY, ANY] + [ANY] * len(saved),
        out_specs=[ANY] * (len(saved) + 1),
        input_output_aliases={11 + q: q for q in range(len(saved))},
        scratch_shapes=[
            pltpu.VMEM((positions, channels), BF16),
            pltpu.VMEM(pad_shape, F32),
            pltpu.VMEM((positions, channels), F32),
            pltpu.VMEM((positions, channels), BF16),
            pltpu.VMEM((positions, LANES), F32),
            pltpu.VMEM((channels, width), BF16),
            pltpu.VMEM((width, channels), BF16),
            pltpu.VMEM((positions, width), BF16),
            pltpu.VMEM((positions, width), BF16),
            pltpu.VMEM((positions, channels), F32),
            pltpu.VMEM((positions, channels), BF16),
            pltpu.VMEM((positions, channels), BF16),
            pltpu.VMEM((positions, channels), BF16),
            pltpu.SemaphoreType.DMA((10,)),
            pltpu.SemaphoreType.DMA((6,)),
        ],
        compiler_params=PARAMS,
        name="block_backward",
    )
    made = blank((*kept, one, *saved, one))
    stash, received = tuple(made[: len(kept)]), made[len(kept)]
    grads, returned = tuple(made[len(kept) + 1 : -1]), made[-1]
    route = [(i, i + 1) for i in range(sections - 1)]
    back_route = [(i + 1, i) for i in range(sections - 1)]
    ticks = micro + sections - 1
    order = owner_order(lax.axis_index("dp"))
    place = jnp.stack([section, sections - 1 - section]).astype(jnp.int32)

    def forward_tick(tick, received, stash):
        *stash, y = forward_call(
            tick.reshape(1), place, roster, received, images, taps, layer_scale, up, down, *stash
        )
        return tuple(stash), y

    def forward_loop(tick, state):
        received, stash = state
        stash, y = forward_tick(tick, received, stash)
        return lax.ppermute(y, "section", route), stash

    received, stash = lax.fori_loop(0, ticks - 1, forward_loop, (received, stash))
    stash, _ = forward_tick(jnp.int32(ticks - 1), received, stash)
    outputs, x_s, n_s, istd_s, hid_s, slope_s, branch_s = stash

    def backward_tick(tick, returned, grads):
        *grads, g = backward_call(
            tick.reshape(1), place, returned, cotangent, taps, layer_scale, up, down, n_s, istd_s, slope_s, *grads
        )
        return tuple(grads), g

    def backward_loop(tick, state):
        returned, grads = state
        grads, g = backward_tick(tick, returned, grads)
        return lax.ppermute(g, "section", back_route), grads

    returned, grads = lax.fori_loop(0, ticks - 1, backward_loop, (returned, grads))
    grads, _ = backward_tick(jnp.int32(ticks - 1), returned, grads)
    go_s, gp_s, gc_s = grads

    real_rows = (side * side * channels + 2 * channels * width + channels) // LANES
    slot_count = master.shape[1]
    share = -(-slot_count // 16) * 16
    buckets = bucket_owner.shape[1]
    cut = share * 4 // 7 // 32 * 32 + share % 32
    pieces = pl.pallas_call(
        functools.partial(
            weight_kernel, (*dims, real_rows, replicas, buckets, share, cut)
        ),
        out_shape=tuple(sds(shape, BF16) for shape in piece_shapes(share, cut)),
        in_specs=[SMEM, SMEM, SMEM, VMEM] + [ANY] * 7,
        out_specs=[ANY] * PIECES,
        scratch_shapes=[
            pltpu.VMEM((micro * positions, channels), BF16),
            pltpu.VMEM((micro * positions, channels), BF16),
            pltpu.VMEM((micro * positions, width), BF16),
            pltpu.VMEM((micro * positions, channels), BF16),
            pltpu.VMEM((micro * positions, channels), BF16),
            pltpu.VMEM((micro * positions, width), BF16),
            pltpu.VMEM((micro * positions, channels), BF16),
            pltpu.VMEM((micro * positions, channels), BF16),
            pltpu.VMEM(pad_shape, F32),
            pltpu.VMEM((-(-real_rows // replicas) * replicas + STEP, LANES), F32),
            pltpu.VMEM((share + 2 * STEP, LANES), F32),
            pltpu.VMEM((2, share, LANES), BF16),
            pltpu.SMEM((buckets,), jnp.int32),
            pltpu.SMEM((buckets,), jnp.int32),
            pltpu.SMEM((replicas,), jnp.int32),
            pltpu.SemaphoreType.DMA((7 * micro + 6,)),
        ],
        compiler_params=PARAMS,
        name="weight_grads",
    )(
        bucket_bounds[0], bucket_owner[0], order, layer_scale, x_s, n_s, hid_s, branch_s, go_s, gp_s, gc_s
    )
    summed = jnp.concatenate([plus(*values) for values in relay_sum(pieces)])
    quads = slot_count // 4
    count = 67 if quads % 67 == 0 else 1
    part = pl.BlockSpec((count, 4, LANES), lambda i: (i, 0, 0))
    quad = sds((quads, 4, LANES), F32)
    new = pl.pallas_call(
        functools.partial(adam_kernel, count, replicas),
        grid=(quads // count,),
        out_shape=(quad, quad, quad),
        in_specs=[pl.BlockSpec((share, LANES), lambda i: (0, 0)), part, part, part],
        out_specs=[part, part, part],
        scratch_shapes=[pltpu.VMEM((share, LANES), F32)],
        compiler_params=pltpu.CompilerParams(vmem_limit_bytes=16 * 1024 * 1024),
        name="adam",
    )(
        summed,
        master.reshape(quads, 4, LANES),
        first_moment.reshape(quads, 4, LANES),
        second_moment.reshape(quads, 4, LANES),
    )
    new_master, new_first, new_second = (value.reshape(master.shape) for value in new)
    return (
        outputs.reshape(1, micro, height, breadth, channels),
        new_master,
        new_first,
        new_second,
    )


def solution(mesh):
    placed = (
        P("dp", None, None, None),
        P("dp", None),
        P("dp", None, None, None),
        P("section", None, None, None),
        P("section", None, None),
        P("section", None, None),
        P("section", None),
        P("section", "dp", None),
        P("section", "dp", None),
        P("section", "dp", None),
        P("section", None),
        P("section", None),
    )
    return jax.shard_map(
        body,
        mesh=mesh,
        in_specs=placed,
        out_specs=(
            P("section", "dp", None, None, None),
            P("section", "dp", None),
            P("section", "dp", None),
            P("section", "dp", None),
        ),
        check_vma=False,
    )
```

```python
import functools

import jax
import jax.numpy as jnp
from jax import lax
from jax.experimental import pallas as pl
from jax.experimental.pallas import tpu as pltpu
from jax.sharding import PartitionSpec as P

beta_one = 0.9
beta_two = 0.95
learn_rate = 0.01
decay_rate = 0.1
adam_eps = 1e-08
norm_eps = 1e-06
first_fix = 1.0 - 0.9**10
second_fix = 1.0 - 0.95**10

LANES = 128
MARGIN = 8
STEP = 64
SLICE = 512
F32 = jnp.float32
BF16 = jnp.bfloat16
ANY = pl.BlockSpec(memory_space=pl.ANY)
SMEM = pl.BlockSpec(memory_space=pltpu.SMEM)
VMEM = pl.BlockSpec(memory_space=pltpu.VMEM)
PARAMS = pltpu.CompilerParams(vmem_limit_bytes=56 * 1024 * 1024)


def rolled(count):
    def wrap(fn):
        lax.fori_loop(0, count, lambda i, c: (fn(i), c)[1], 0)

    return wrap


def pad_map(pad, image, reach, height, breadth):
    chunks = pad.shape[0]
    for c in range(chunks):
        for r in range(pad.shape[1]):
            if r < reach or r >= reach + height:
                pad[c, r] = jnp.zeros(pad.shape[2:], F32)
            else:
                pad[c, r, :MARGIN] = jnp.zeros((MARGIN, LANES), F32)
                pad[c, r, MARGIN + breadth :] = jnp.zeros((MARGIN, LANES), F32)
                pad[c, r, MARGIN : MARGIN + breadth] = image[
                    (r - reach) * breadth : (r - reach + 1) * breadth,
                    c * LANES : (c + 1) * LANES,
                ].astype(F32)


def depthwise(pad, taps, result, side, height, breadth, flip):
    reach = (side - 1) // 2
    halves = breadth // 8

    @rolled(pad.shape[0])
    def _(c):
        sums = [[None] * halves for _ in range(height)]
        for b in range(side):
            weights = []
            for a in range(side):
                t = a * side + b
                t = side * side - 1 - t if flip else t
                weights.append(jnp.broadcast_to(taps[c, pl.ds(t, 1), :], (8, LANES)))
            for r in range(height + 2 * reach):
                for w in range(halves):
                    value = pad[c, r, pl.ds(MARGIN - reach + b + 8 * w, 8), :]
                    for a in range(side):
                        i = r - a
                        if 0 <= i < height:
                            term = value * weights[a]
                            sums[i][w] = term if sums[i][w] is None else sums[i][w] + term
        columns = pl.ds(pl.multiple_of(c * LANES, LANES), LANES)
        for i in range(height):
            for w in range(halves):
                result[pl.ds(i * breadth + 8 * w, 8), columns] = sums[i][w]


class Streamed:
    def __init__(self, up, upv, down, downv, slope, slopev, sems):
        half = up.shape[1] // 2
        self.parts = []
        for q in range(2):
            cut = pl.ds(q * half, half)
            self.parts.append(
                (
                    pltpu.make_async_copy(down.at[cut], downv.at[cut], sems.at[3 * q]),
                    pltpu.make_async_copy(slope.at[:, cut], slopev.at[:, cut], sems.at[3 * q + 1]),
                    pltpu.make_async_copy(up.at[:, cut], upv.at[:, cut], sems.at[3 * q + 2]),
                )
            )

    def start(self):
        for part in self.parts:
            for cp in part:
                cp.start()

    def wait(self, q):
        for cp in self.parts[q]:
            cp.wait()


def forward_kernel(
    dims, tick, place, roster, xr, images, taps, scale, up, down, *refs
):
    side, height, breadth, width = dims
    out_o, x_o, n_o, istd_o, hid_o, slope_o, branch_o, y = refs[7:15]
    xv, pad, conv, nv, iv, upv, downv, hv, sv, acc, bv, yv, sems = refs[15:]
    positions, channels = xv.shape
    micro = images.shape[0]
    reach = (side - 1) // 2
    slot = tick[0] - place[0]

    @pl.when((slot >= 0) & (slot < micro))
    def _():
        up_in = pltpu.make_async_copy(up, upv, sems.at[0])
        down_in = pltpu.make_async_copy(down, downv, sems.at[1])

        @pl.when(place[0] == 0)
        def _():
            cp = pltpu.make_async_copy(images.at[roster[0, slot]], xv, sems.at[2])
            cp.start()
            up_in.start()
            down_in.start()
            cp.wait()

        @pl.when(place[0] > 0)
        def _():
            cp = pltpu.make_async_copy(xr, xv, sems.at[2])
            cp.start()
            up_in.start()
            down_in.start()
            cp.wait()

        x_out = pltpu.make_async_copy(xv, x_o.at[slot], sems.at[3])
        x_out.start()
        pad_map(pad, xv, reach, height, breadth)
        depthwise(pad, taps, conv, side, height, breadth, False)
        block = 64
        for p in range(0, positions, block):
            rows = conv[p : p + block, :]
            centred = rows - jnp.mean(rows, axis=-1, keepdims=True)
            inv_std = lax.rsqrt(jnp.mean(centred * centred, axis=-1, keepdims=True) + norm_eps)
            nv[p : p + block, :] = (centred * inv_std).astype(BF16)
            iv[p : p + block, :] = jnp.broadcast_to(inv_std, (block, LANES))
        n_out = pltpu.make_async_copy(nv, n_o.at[slot], sems.at[4])
        n_out.start()
        i_out = pltpu.make_async_copy(iv, istd_o.at[slot], sems.at[5])
        i_out.start()
        up_in.wait()
        down_in.wait()
        step = 512
        for k in range(0, width, step):
            pre = jnp.dot(nv[...], upv[:, k : k + step], preferred_element_type=F32)
            cdf = 0.5 * (1.0 + lax.erf(pre * 0.7071067811865476))
            hidden = (pre * cdf).astype(BF16)
            hv[:, k : k + step] = hidden
            bell = jnp.exp(-0.5 * pre * pre) * 0.3989422804014327
            sv[:, k : k + step] = (cdf + pre * bell).astype(BF16)
            part = jnp.dot(hidden, downv[k : k + step, :], preferred_element_type=F32)
            if k == 0:
                acc[...] = part
            else:
                acc[...] += part
        yv[...] = (xv[...].astype(F32) + scale[...] * acc[...]).astype(BF16)
        y_out = pltpu.make_async_copy(yv, y, sems.at[6])
        y_out.start()
        o_out = pltpu.make_async_copy(yv, out_o.at[slot], sems.at[7])
        o_out.start()
        h_out = pltpu.make_async_copy(hv, hid_o.at[slot], sems.at[8])
        h_out.start()
        s_out = pltpu.make_async_copy(sv, slope_o.at[slot], sems.at[9])
        s_out.start()
        bv[...] = acc[...].astype(BF16)
        b_out = pltpu.make_async_copy(bv, branch_o.at[slot], sems.at[10])
        b_out.start()
        for cp in (x_out, n_out, i_out, y_out, o_out, h_out, s_out, b_out):
            cp.wait()


def backward_kernel(
    dims, tick, place, gr, cotangent, taps, scale, up, down, n_i, istd_i, slope_i, *refs
):
    side, height, breadth, width = dims
    go_o, gp_o, gc_o, g_in = refs[3:7]
    gv, pad, conv, nv, iv, upv, downv, sv, gpv, acc, scaled, gcv, yv, sems, weight_sems = refs[7:]
    positions, channels = gv.shape
    micro = cotangent.shape[0]
    reach = (side - 1) // 2
    slot = tick[0] - place[1]

    @pl.when((slot >= 0) & (slot < micro))
    def _():
        weights = Streamed(up, upv, down, downv, slope_i.at[slot], sv, weight_sems)
        n_in = pltpu.make_async_copy(n_i.at[slot], nv, sems.at[4])
        i_in = pltpu.make_async_copy(istd_i.at[slot], iv, sems.at[5])

        def begin(source):
            cp = pltpu.make_async_copy(source, gv, sems.at[2])
            cp.start()
            weights.start()
            n_in.start()
            i_in.start()
            cp.wait()

        @pl.when(place[1] == 0)
        def _():
            begin(cotangent.at[slot])

        @pl.when(place[1] > 0)
        def _():
            begin(gr)

        go_out = pltpu.make_async_copy(gv, go_o.at[slot], sems.at[6])
        go_out.start()
        scaled[...] = (gv[...].astype(F32) * scale[...]).astype(BF16)
        step = SLICE
        across = (((1,), (1,)), ((), ()))
        for k in range(0, width, step):
            if k % (width // 2) == 0:
                weights.wait(k // (width // 2))
            grad_hidden = lax.dot_general(
                scaled[...], downv[k : k + step, :], across, preferred_element_type=F32
            )
            grad_pre = (grad_hidden * sv[:, k : k + step].astype(F32)).astype(BF16)
            gpv[:, k : k + step] = grad_pre
            part = lax.dot_general(
                grad_pre, upv[:, k : k + step], across, preferred_element_type=F32
            )
            if k == 0:
                acc[...] = part
            else:
                acc[...] += part
        gp_out = pltpu.make_async_copy(gpv, gp_o.at[slot], sems.at[7])
        gp_out.start()
        n_in.wait()
        i_in.wait()
        block = 64
        for p in range(0, positions, block):
            rows = acc[p : p + block, :]
            normed = nv[p : p + block, :].astype(F32)
            mean = jnp.mean(rows, axis=-1, keepdims=True)
            slant = jnp.mean(rows * normed, axis=-1, keepdims=True)
            gcv[p : p + block, :] = (
                iv[p : p + block, :1] * (rows - mean - normed * slant)
            ).astype(BF16)
        gc_out = pltpu.make_async_copy(gcv, gc_o.at[slot], sems.at[8])
        gc_out.start()

        @pl.when(place[0] > 0)
        def _():
            pad_map(pad, gcv, reach, height, breadth)
            depthwise(pad, taps, conv, side, height, breadth, True)
            yv[...] = (gv[...].astype(F32) + conv[...]).astype(BF16)
            cp = pltpu.make_async_copy(yv, g_in, sems.at[9])
            cp.start()
            cp.wait()

        for cp in (go_out, gp_out, gc_out):
            cp.wait()


def weight_kernel(
    dims, bounds, owners, order, scale, x_i, n_i, hid_i, branch_i, go_i, gp_i, gc_i, *refs
):
    side, height, breadth, width, real_rows, owner_count, buckets, share, cut = dims
    pieces, refs = refs[:PIECES], refs[PIECES:]
    (xv, nv, hv, bv, gv, gpv, gcv, scaled, pad, flat, stage, ready, starts, lengths, counts, sems) = refs
    micro, positions, channels = x_i.shape
    reach = (side - 1) // 2
    chunks = channels // LANES
    rows = micro * positions
    tap_rows = side * side * chunks
    up_rows = channels * (width // LANES)
    down_base = tap_rows + up_rows
    scale_base = down_base + up_rows
    copies = []
    for q, (src, dst) in enumerate(
        ((x_i, xv), (gc_i, gcv), (n_i, nv), (gp_i, gpv), (go_i, gv), (hid_i, hv), (branch_i, bv))
    ):
        for m in range(micro):
            cp = pltpu.make_async_copy(
                src.at[m], dst.at[pl.ds(m * positions, positions)], sems.at[q * micro + m]
            )
            cp.start()
            copies.append(cp)
    for d in range(owner_count):
        counts[d] = 0

    @rolled(buckets)
    def _(b):
        d = owners[b]
        at = d * (buckets // owner_count) + counts[d]
        starts[at] = bounds[b]
        lengths[at] = bounds[b + 1] - bounds[b]
        counts[d] = counts[d] + 1

    early = 2 * micro
    for cp in copies[:early]:
        cp.wait()
    halves = breadth // 8
    flat[:tap_rows, :] = jnp.zeros((tap_rows, LANES), F32)

    @rolled(micro)
    def _(m):
        base = pl.multiple_of(m * positions, positions)
        pad_map(pad, xv.at[pl.ds(base, positions)], reach, height, breadth)

        @rolled(chunks)
        def _(c):
            columns = pl.ds(pl.multiple_of(c * LANES, LANES), LANES)
            grads = [
                gcv[pl.ds(base + 16 * i, 16), columns].astype(F32)
                for i in range(positions // 16)
            ]
            for b in range(side):
                sums = [None] * side
                for r in range(reach, height + reach):
                    for w in range(halves):
                        value = pad[c, r, pl.ds(MARGIN - reach + b + 8 * w, 8), :]
                        for a in range(side):
                            i = r - a
                            if 0 <= i < height:
                                p = i * breadth + 8 * w
                                term = value * grads[p // 16][p % 16 : p % 16 + 8]
                                sums[a] = term if sums[a] is None else sums[a] + term
                for a in range(side):
                    total = jnp.sum(sums[a], axis=0, keepdims=True)
                    at = pl.ds((a * side + b) * chunks + c, 1)
                    flat[at, :] += total

    for cp in copies[early:]:
        cp.wait()
    along = (((0,), (0,)), ((), ()))
    scaled[...] = (gv[...].astype(F32) * scale[...]).astype(BF16)
    for j in range(0, width // LANES, 2):
        part = lax.dot_general(
            nv[...], gpv[:, j * LANES : (j + 2) * LANES], along, preferred_element_type=F32
        )
        for q in range(2):
            flat[pl.ds(tap_rows + j + q, channels, stride=width // LANES), :] = part[
                :, q * LANES : (q + 1) * LANES
            ]
    for j in range(0, chunks, 2):
        part = lax.dot_general(
            hv[...], scaled[:, j * LANES : (j + 2) * LANES], along, preferred_element_type=F32
        )
        for q in range(2):
            flat[pl.ds(down_base + j + q, width, stride=chunks), :] = part[
                :, q * LANES : (q + 1) * LANES
            ]
    terms = jnp.sum(gv[...].astype(F32) * bv[...].astype(F32), axis=0, keepdims=True)
    for c in range(chunks):
        flat[pl.ds(scale_base + c, 1), :] = terms[:, c * LANES : (c + 1) * LANES]
    tail = flat.shape[0] - scale_base - chunks
    flat[pl.ds(scale_base + chunks, tail), :] = jnp.zeros((tail, LANES), F32)
    half = (share - cut) // 2
    spans = ((0, cut), (cut, half), (cut + half, half))

    def out_copies(target, q, n):
        result = []
        for part, (first, size) in enumerate(spans):
            piece, at = target[part]
            result.append(
                pltpu.make_async_copy(
                    ready.at[q, pl.ds(first, size)],
                    pieces[piece].at[at],
                    sems.at[7 * micro + 3 * q + part],
                )
            )
        return result

    waiting = [None, None]
    for n, target in enumerate(relay_targets()):
        q = n % 2
        d = order[n]
        offset = 0
        for k in range(buckets // owner_count):
            at = d * (buckets // owner_count) + k
            start, length = starts[at], lengths[at]
            here = offset

            def move(i, c, start=start, here=here):
                stage[pl.ds(here + STEP * i, STEP), :] = flat[pl.ds(start + STEP * i, STEP), :]
                return c

            lax.fori_loop(0, lax.div(length + STEP - 1, STEP), move, 0)
            offset = offset + length

        def clear(i, c, offset=offset):
            stage[pl.ds(offset + STEP * i, STEP), :] = jnp.zeros((STEP, LANES), F32)
            return c

        lax.fori_loop(0, lax.div(share - offset + STEP - 1, STEP), clear, 0)
        if waiting[q] is not None:
            for cp in waiting[q]:
                cp.wait()
        ready[q] = stage[:share, :].astype(BF16)
        waiting[q] = out_copies(target, q, n)
        for cp in waiting[q]:
            cp.start()
    for q in range(2):
        for cp in waiting[q]:
            cp.wait()


ORBIT = 4
PIECES = 12


def relay_order():
    order = []
    for core in (1, 0):
        for z, x in ((0, 3), (1, 1), (0, 2), (1, 2), (0, 1), (1, 3), (0, 0), (1, 0)):
            order.append((core, z, x))
    return order


def relay_targets():
    turn = {(0, 3): 0, (1, 1): 0, (0, 2): 1, (1, 2): 1, (0, 1): 2, (1, 3): 2, (0, 0): 3, (1, 0): 3}
    result = []
    for core, z, x in relay_order():
        base = 6 * (1 - core)
        q = base + 4 + (1 - z)
        result.append(((base + turn[z, x], z), (q, x), (q, ORBIT + x)))
    return result


def piece_shapes(share, cut):
    half = (share - cut) // 2
    one = [(2, cut, LANES)] * 4 + [(2 * ORBIT, half, LANES)] * 2
    return one + one


def owner_order(me):
    z, x, core = me // 8, (me // 2) % 4, me % 2
    return jnp.stack(
        [((z + dz) % 2) * 8 + ((x + dx) % 4) * 2 + (core + dc) % 2 for dc, dz, dx in relay_order()]
    ).astype(jnp.int32)


def routes():
    def route(to):
        pairs = []
        for me in range(16):
            z, x, core = me // 8, (me // 2) % 4, me % 2
            z, x, core = to(z, x, core)
            pairs.append((me, z * 8 + x * 2 + core))
        return pairs

    return (
        route(lambda z, x, c: (z, x, 1 - c)),
        route(lambda z, x, c: (z, (x + 1) % 4, c)),
        route(lambda z, x, c: (z, (x + 3) % 4, c)),
        route(lambda z, x, c: (1 - z, x, c)),
    )


def plus(*values):
    total = values[0].astype(F32)
    for value in values[1:]:
        total = total + value.astype(F32)
    return total.astype(BF16)


def relay_sum(pieces):
    across, right, left, over = routes()
    sent, kept = pieces[:6], pieces[6:]
    half = sent[4].shape[1]

    def hop(value, route):
        return lax.ppermute(value, "dp", route)

    came = [None] * 6
    for q in (0, 4, 1, 2, 5, 3):
        came[q] = hop(sent[q], across)
    r = hop(plus(kept[0][0], came[0][0]), right)
    l = hop(plus(kept[0][1], came[0][1]), left)
    far = hop(plus(kept[4][:ORBIT], came[4][:ORBIT]), over)
    farther = hop(plus(kept[4][ORBIT:], came[4][ORBIT:]), over)
    for q in (1, 2):
        r = hop(plus(kept[q][0], came[q][0], r), right)
        l = hop(plus(kept[q][1], came[q][1], l), left)
    z_sent = hop(plus(kept[3][1], came[3][1], l), over)
    near = (kept[5][:ORBIT], came[5][:ORBIT], far)
    nearer = (kept[5][ORBIT:], came[5][ORBIT:], farther)
    a = hop(plus(*(v[3] for v in near)), right)
    b = hop(plus(*(v[1] for v in nearer)), left)
    for step in (2, 1):
        a = hop(plus(*(v[step] for v in near), a), right)
        b = hop(plus(*(v[4 - step] for v in nearer), b), left)
    first = (kept[3][0], came[3][0], r, z_sent)
    return first, tuple(v[0] for v in near) + (a,), tuple(v[0] for v in nearer) + (b,)


def adam_kernel(count, replicas, g_i, m_i, f_i, s_i, m_o, f_o, s_o, grads):
    @pl.when(pl.program_id(0) == 0)
    def _():
        grads[...] = g_i[...].astype(F32) * (1.0 / replicas)

    base = pl.program_id(0) * (4 * count)
    for k in range(count):
        grad = grads[pl.ds(base + 4 * k, 4), :]
        new_first = beta_one * f_i[k] + (1.0 - beta_one) * grad
        new_second = beta_two * s_i[k] + (1.0 - beta_two) * grad * grad
        update = (
            new_first / first_fix / (jnp.sqrt(new_second / second_fix) + adam_eps)
            + decay_rate * m_i[k]
        )
        m_o[k] = m_i[k] - learn_rate * update
        f_o[k] = new_first
        s_o[k] = new_second


def blank(shapes):
    def kernel(*refs):
        pass

    return pl.pallas_call(
        kernel, out_shape=shapes, out_specs=[ANY] * len(shapes), name="blank"
    )()


def body(
    images,
    roster,
    cotangent,
    depth_kernel,
    up_weight,
    down_weight,
    layer_scale,
    master,
    first_moment,
    second_moment,
    bucket_bounds,
    bucket_owner,
):
    sections = lax.axis_size("section")
    replicas = lax.axis_size("dp")
    section = lax.axis_index("section")
    micro, height, breadth, channels = images.shape
    side = depth_kernel.shape[1]
    width = up_weight.shape[2]
    positions = height * breadth
    chunks = channels // LANES
    up, down = up_weight[0], down_weight[0]
    taps = (
        depth_kernel[0].astype(F32).reshape(side * side, chunks, LANES).transpose(1, 0, 2)
    )
    images = images.reshape(micro, positions, channels)
    cotangent = cotangent.reshape(micro, positions, channels)
    sds = jax.ShapeDtypeStruct
    act = sds((micro, positions, channels), BF16)
    wide = sds((micro, positions, width), BF16)
    one = sds((positions, channels), BF16)
    spread = sds((micro, positions, LANES), F32)
    full = sds((micro, positions, channels), BF16)
    pad_shape = (chunks, height + side - 1, breadth + 2 * MARGIN, LANES)
    dims = (side, height, breadth, width)

    kept = (act, act, act, spread, wide, wide, full)
    forward_call = pl.pallas_call(
        functools.partial(forward_kernel, dims),
        out_shape=(*kept, one),
        in_specs=[SMEM, SMEM, SMEM, ANY, ANY, VMEM, VMEM, ANY, ANY] + [ANY] * len(kept),
        out_specs=[ANY] * (len(kept) + 1),
        input_output_aliases={9 + q: q for q in range(len(kept))},
        scratch_shapes=[
            pltpu.VMEM((positions, channels), BF16),
            pltpu.VMEM(pad_shape, F32),
            pltpu.VMEM((positions, channels), F32),
            pltpu.VMEM((positions, channels), BF16),
            pltpu.VMEM((positions, LANES), F32),
            pltpu.VMEM((channels, width), BF16),
            pltpu.VMEM((width, channels), BF16),
            pltpu.VMEM((positions, width), BF16),
            pltpu.VMEM((positions, width), BF16),
            pltpu.VMEM((positions, channels), F32),
            pltpu.VMEM((positions, channels), BF16),
            pltpu.VMEM((positions, channels), BF16),
            pltpu.SemaphoreType.DMA((11,)),
        ],
        compiler_params=PARAMS,
        name="block_forward",
    )
    saved = (act, wide, act)
    backward_call = pl.pallas_call(
        functools.partial(backward_kernel, dims),
        out_shape=(*saved, one),
        in_specs=[SMEM, SMEM, ANY, ANY, VMEM, VMEM, ANY, ANY, ANY, ANY, ANY] + [ANY] * len(saved),
        out_specs=[ANY] * (len(saved) + 1),
        input_output_aliases={11 + q: q for q in range(len(saved))},
        scratch_shapes=[
            pltpu.VMEM((positions, channels), BF16),
            pltpu.VMEM(pad_shape, F32),
            pltpu.VMEM((positions, channels), F32),
            pltpu.VMEM((positions, channels), BF16),
            pltpu.VMEM((positions, LANES), F32),
            pltpu.VMEM((channels, width), BF16),
            pltpu.VMEM((width, channels), BF16),
            pltpu.VMEM((positions, width), BF16),
            pltpu.VMEM((positions, width), BF16),
            pltpu.VMEM((positions, channels), F32),
            pltpu.VMEM((positions, channels), BF16),
            pltpu.VMEM((positions, channels), BF16),
            pltpu.VMEM((positions, channels), BF16),
            pltpu.SemaphoreType.DMA((10,)),
            pltpu.SemaphoreType.DMA((6,)),
        ],
        compiler_params=PARAMS,
        name="block_backward",
    )
    made = blank((*kept, one, *saved, one))
    stash, received = tuple(made[: len(kept)]), made[len(kept)]
    grads, returned = tuple(made[len(kept) + 1 : -1]), made[-1]
    route = [(i, i + 1) for i in range(sections - 1)]
    back_route = [(i + 1, i) for i in range(sections - 1)]
    ticks = micro + sections - 1
    order = owner_order(lax.axis_index("dp"))
    place = jnp.stack([section, sections - 1 - section]).astype(jnp.int32)

    def forward_tick(tick, received, stash):
        *stash, y = forward_call(
            tick.reshape(1), place, roster, received, images, taps, layer_scale, up, down, *stash
        )
        return tuple(stash), y

    def forward_loop(tick, state):
        received, stash = state
        stash, y = forward_tick(tick, received, stash)
        return lax.ppermute(y, "section", route), stash

    received, stash = lax.fori_loop(0, ticks - 1, forward_loop, (received, stash))
    stash, _ = forward_tick(jnp.int32(ticks - 1), received, stash)
    outputs, x_s, n_s, istd_s, hid_s, slope_s, branch_s = stash

    def backward_tick(tick, returned, grads):
        *grads, g = backward_call(
            tick.reshape(1), place, returned, cotangent, taps, layer_scale, up, down, n_s, istd_s, slope_s, *grads
        )
        return tuple(grads), g

    def backward_loop(tick, state):
        returned, grads = state
        grads, g = backward_tick(tick, returned, grads)
        return lax.ppermute(g, "section", back_route), grads

    returned, grads = lax.fori_loop(0, ticks - 1, backward_loop, (returned, grads))
    grads, _ = backward_tick(jnp.int32(ticks - 1), returned, grads)
    go_s, gp_s, gc_s = grads

    real_rows = (side * side * channels + 2 * channels * width + channels) // LANES
    slot_count = master.shape[1]
    share = -(-slot_count // 16) * 16
    buckets = bucket_owner.shape[1]
    cut = share - share * 3 // 10 // 32 * 32
    pieces = pl.pallas_call(
        functools.partial(
            weight_kernel, (*dims, real_rows, replicas, buckets, share, cut)
        ),
        out_shape=tuple(sds(shape, BF16) for shape in piece_shapes(share, cut)),
        in_specs=[SMEM, SMEM, SMEM, VMEM] + [ANY] * 7,
        out_specs=[ANY] * PIECES,
        scratch_shapes=[
            pltpu.VMEM((micro * positions, channels), BF16),
            pltpu.VMEM((micro * positions, channels), BF16),
            pltpu.VMEM((micro * positions, width), BF16),
            pltpu.VMEM((micro * positions, channels), BF16),
            pltpu.VMEM((micro * positions, channels), BF16),
            pltpu.VMEM((micro * positions, width), BF16),
            pltpu.VMEM((micro * positions, channels), BF16),
            pltpu.VMEM((micro * positions, channels), BF16),
            pltpu.VMEM(pad_shape, F32),
            pltpu.VMEM((-(-real_rows // replicas) * replicas + STEP, LANES), F32),
            pltpu.VMEM((share + 2 * STEP, LANES), F32),
            pltpu.VMEM((2, share, LANES), BF16),
            pltpu.SMEM((buckets,), jnp.int32),
            pltpu.SMEM((buckets,), jnp.int32),
            pltpu.SMEM((replicas,), jnp.int32),
            pltpu.SemaphoreType.DMA((7 * micro + 6,)),
        ],
        compiler_params=PARAMS,
        name="weight_grads",
    )(
        bucket_bounds[0], bucket_owner[0], order, layer_scale, x_s, n_s, hid_s, branch_s, go_s, gp_s, gc_s
    )
    summed = jnp.concatenate([plus(*values) for values in relay_sum(pieces)])
    quads = slot_count // 4
    count = 67 if quads % 67 == 0 else 1
    part = pl.BlockSpec((count, 4, LANES), lambda i: (i, 0, 0))
    quad = sds((quads, 4, LANES), F32)
    new = pl.pallas_call(
        functools.partial(adam_kernel, count, replicas),
        grid=(quads // count,),
        out_shape=(quad, quad, quad),
        in_specs=[pl.BlockSpec((share, LANES), lambda i: (0, 0)), part, part, part],
        out_specs=[part, part, part],
        scratch_shapes=[pltpu.VMEM((share, LANES), F32)],
        compiler_params=pltpu.CompilerParams(vmem_limit_bytes=16 * 1024 * 1024),
        name="adam",
    )(
        summed,
        master.reshape(quads, 4, LANES),
        first_moment.reshape(quads, 4, LANES),
        second_moment.reshape(quads, 4, LANES),
    )
    new_master, new_first, new_second = (value.reshape(master.shape) for value in new)
    return (
        outputs.reshape(1, micro, height, breadth, channels),
        new_master,
        new_first,
        new_second,
    )


def solution(mesh):
    placed = (
        P("dp", None, None, None),
        P("dp", None),
        P("dp", None, None, None),
        P("section", None, None, None),
        P("section", None, None),
        P("section", None, None),
        P("section", None),
        P("section", "dp", None),
        P("section", "dp", None),
        P("section", "dp", None),
        P("section", None),
        P("section", None),
    )
    return jax.shard_map(
        body,
        mesh=mesh,
        in_specs=placed,
        out_specs=(
            P("section", "dp", None, None, None),
            P("section", "dp", None),
            P("section", "dp", None),
            P("section", "dp", None),
        ),
        check_vma=False,
    )
```
